256 devices in a mesh: section: 8 (over y, core), row: 32 (over z, x).
Axes of the slice: x: 4, y: 4, z: 8, core: 2. Of those that a mesh axis runs over, the one named last changes fastest.
Arguments:
- channel_rows_in: bfloat16 [1024, 32, 4096], P('row', None, 'section'), may hold values from -6 to 6
- gate_rows_in: bfloat16 [1024, 32, 4096], P('row', None, 'section'), may hold values from -6 to 6
- map_input_rows: bfloat16 [1024, 32, 256], P('row'), may hold values from -6 to 6
- step_size_input: bfloat16 [1024, 64, 32], P('row', 'section'), may hold values from -4 to 4
- channel_kernel_weight: float32 [4, 4096], P(None, 'section'), may hold values from -3 to 3
- map_kernel_weight: float32 [4, 256], replicated, may hold values from -3 to 3
- channel_conv_bias: float32 [4096], P('section'), may hold values from -3 to 3
- map_kernel_bias: float32 [256], replicated, may hold values from -3 to 3
- step_size_bias: float32 [64], P('section'), may hold values from -2 to 0
- head_decay_rate: float32 [64], P('section'), may hold values from 0.003 to 1
- head_skip_weight: float32 [64], P('section'), may hold values from 0.5 to 1.5
- gated_norm_scale: float32 [4096], P('section'), may hold values from 0.5 to 1.5
- scan_state_cache: bfloat16 [1024, 64, 64, 128], P('row', 'section'), may hold values from -2 to 2
- channel_window_cache: bfloat16 [1024, 3, 4096], P('row', None, 'section'), may hold values from -6 to 6
- map_window_cache: bfloat16 [1024, 3, 256], P('row'), may hold values from -6 to 6
- adapter_down_weight: bfloat16 [32, 64, 4096], P('row', None, 'section'), may hold values from -0.09375 to 0.09375
- adapter_up_weight: bfloat16 [32, 64, 4096], P('row', None, 'section'), may hold values from -0.75 to 0.75
- session_slot_index: int32 [1024], replicated, may hold values from 0 to 1023, as said below
- lengths: int32 [1024], replicated, may hold values from 1 to 32
- session_adapter_index: int32 [1024], replicated, may hold values from 0 to 31
Outputs:
- mixer_output_rows: bfloat16 [1024, 32, 4096], P('row', None, 'section')
- adapter_delta: bfloat16 [1024, 32, 4096], P('row', None, 'section')
- scan_state_next: bfloat16 [1024, 64, 64, 128], P('row', 'section')
- channel_window_next: bfloat16 [1024, 3, 4096], P('row', None, 'section')
- map_window_next: bfloat16 [1024, 3, 256], P('row')
The draws below stay inside these ranges and needn't reach their ends.
Inputs may be any that keep to these rules, and one draw needn't show every extreme that they name: `session_slot_index`: A permutation of the 1024 cache slots; cache slot c lies on row c // 32 and served session q on row q // 32. The states of one serving row's sessions come from exactly 16 home rows, 2 from each, so every home row also sends to that many rows.
All inputs are finite; a program needn't handle non-finite values.
Results may differ from the reference program's by a relative error of at most 0.0058.
Values may be sent and summed in bfloat16 or wider, within the bound.
No kernel may reach another device: no remote copies, remote signals or barrier semaphores. Data moves between devices by JAX's collectives and lax.ppermute only.
A program may use at most 128 MiB of HBM per device.

```python
import math
import jax
import jax.numpy as jnp
import numpy as np
from jax import lax

MODEL_WIDTH = 4096
H = 64
P_SIZE = 64
N = 128
ADAPTER_RANK = 64
TOK_SESS = 32
SLOTS_DEV = 32
INNER_CHANNELS = 4096
SESSIONS = 1024
ADAPTER_TOTAL = 32
MOST = 2


def draw_session_slot_index(key, part):
    row_total = SESSIONS // SLOTS_DEV
    group_count = SLOTS_DEV // MOST
    subkeys = jax.random.split(key, 4)
    offsets = jax.random.permutation(subkeys[0], row_total)[:group_count]
    slot_offset = jnp.repeat(offsets, MOST)
    relabel = jax.random.permutation(subkeys[1], row_total)
    serving = jnp.arange(row_total)[:, None]
    home_row = relabel[(serving + slot_offset[None, :]) % row_total]
    column = jnp.arange(SLOTS_DEV)[None, :]
    home_scores = jax.random.randint(subkeys[2], (row_total, SLOTS_DEV), 0, 1 << 20) * SLOTS_DEV + column
    home_order = jnp.argsort(home_scores, axis=1)
    home_slot = home_row * SLOTS_DEV + home_order[home_row, column]
    serve_scores = jax.random.randint(subkeys[3], (row_total, SLOTS_DEV), 0, 1 << 20) * SLOTS_DEV + column
    serve_order = jnp.argsort(serve_scores, axis=1)
    shuffled = jnp.take_along_axis(home_slot, serve_order, axis=1)
    return shuffled.reshape(-1).astype(jnp.int32)


def set_ends(entries, key, least, largest):
    dims = entries.shape
    spot = [jax.random.randint(jax.random.fold_in(key, axis), (), 0, dims[axis]) for axis in range(len(dims))]
    entries = entries.at[tuple(spot)].set(least)
    longest = dims.index(max(dims))
    spot[longest] = (spot[longest] + 1) % dims[longest]
    return entries.at[tuple(spot)].set(largest)


def level_of(stream_key, extent, pieces, smallest, high):
    loudness = 1.0
    for position, blocks in pieces:
        draws = jax.random.uniform(jax.random.fold_in(jax.random.fold_in(stream_key, 6), position), (blocks,), jnp.float32, smallest / len(pieces), high / len(pieces))
        loudness = loudness * jnp.repeat(jnp.exp(draws), extent[position] // blocks).reshape((-1,) + (1,) * (len(extent) - 1 - position))
    return loudness


def rank_table(count, slope):
    weights = [(1 << 20) // math.isqrt(grade ** slope) + 1 for grade in range(1, count + 1)]
    scale = 1 + sum(weights) // (1 << 30)
    return np.cumsum(np.array([max(1, weight // scale) for weight in weights]))


def skewed_ids(key, extent, number_of, slope):
    listing = rank_table(number_of, slope)
    ticket = jax.random.randint(jax.random.fold_in(key, 1), extent, 0, int(listing[number_of - 1]))
    standing = jnp.searchsorted(jnp.asarray(listing, jnp.int32), ticket, side="right")
    return jax.random.permutation(jax.random.fold_in(key, 2), number_of)[standing].astype(jnp.int32)


def gaussian(key, extent, scale, bound, shards=(), kind=jnp.bfloat16):
    drawn = scale * jax.random.normal(key, extent, jnp.float32)
    if shards:
        drawn = drawn * level_of(key, extent, shards, -0.22, 0.18)
    return jnp.clip(drawn, -bound, bound).astype(kind)


def setup_inputs(seed: int = 0) -> dict:
    keys = jax.random.split(jax.random.key(seed), 21)
    channel_rows_in = gaussian(keys[0], (SESSIONS, TOK_SESS, INNER_CHANNELS), 1.0, 6.0, ((0, 32), (2, 8)))
    gate_rows_in = gaussian(keys[1], (SESSIONS, TOK_SESS, INNER_CHANNELS), 1.0, 6.0, ((0, 32), (2, 8)))
    map_input_rows = gaussian(keys[2], (SESSIONS, TOK_SESS, 2 * N), 1.0, 6.0, ((0, 32),))
    step_size_input = gaussian(keys[3], (SESSIONS, H, TOK_SESS), 1.0, 4.0, ((0, 32), (1, 8)))
    channel_kernel_weight = gaussian(keys[4], (4, INNER_CHANNELS), 0.5, 3.0, ((1, 8),), jnp.float32)
    map_kernel_weight = gaussian(keys[5], (4, 2 * N), 0.5, 3.0, (), jnp.float32)
    channel_conv_bias = gaussian(keys[6], (INNER_CHANNELS,), 0.5, 3.0, ((0, 8),), jnp.float32)
    map_kernel_bias = gaussian(keys[7], (2 * N,), 0.5, 3.0, (), jnp.float32)
    step_size_bias = jnp.clip(-2.0 + 2.0 * jax.random.uniform(keys[8], (H,), jnp.float32) ** level_of(keys[8], (H,), ((0, 8),), -0.2, 0.2), -2.0, 0.0)
    head_decay_rate = jnp.clip(jnp.exp(math.log(1.0) - 5.809143 * jax.random.uniform(keys[9], (H,), jnp.float32) ** level_of(keys[9], (H,), ((0, 8),), -0.2, 0.2)), 0.003, 1.0)
    head_skip_weight = jnp.clip(0.5 + 1.0 * jax.random.uniform(keys[10], (H,), jnp.float32) ** level_of(keys[10], (H,), ((0, 8),), -0.2, 0.2), 0.5, 1.5)
    gated_norm_scale = jnp.clip(1.0 + 0.1 * jax.random.normal(keys[11], (INNER_CHANNELS,), jnp.float32), 0.5, 1.5)
    scan_state_cache = gaussian(keys[12], (SESSIONS, H, P_SIZE, N), 0.3, 2.0, ((0, 32), (1, 8)))
    channel_window_cache = gaussian(keys[13], (SESSIONS, 3, INNER_CHANNELS), 1.0, 6.0, ((0, 32), (2, 8)))
    map_window_cache = gaussian(keys[14], (SESSIONS, 3, 2 * N), 1.0, 6.0, ((0, 32),))
    adapter_down_weight = gaussian(keys[15], (ADAPTER_TOTAL, ADAPTER_RANK, INNER_CHANNELS), INNER_CHANNELS ** -0.5, 0.09375, ((0, 32), (2, 8)))
    adapter_up_weight = gaussian(keys[16], (ADAPTER_TOTAL, ADAPTER_RANK, MODEL_WIDTH), ADAPTER_RANK ** -0.5, 0.75, ((0, 32), (2, 8)))
    session_slot_index = draw_session_slot_index(jax.random.fold_in(keys[20], 71), 0)
    lengths = set_ends(jax.random.randint(keys[18], (SESSIONS,), 1, TOK_SESS + 1), jax.random.fold_in(keys[18], 1), 1, TOK_SESS).astype(jnp.int32)
    session_adapter_index = set_ends(skewed_ids(keys[19], (SESSIONS,), ADAPTER_TOTAL, 2), jax.random.fold_in(keys[19], 3), 0, ADAPTER_TOTAL - 1).astype(jnp.int32)
    return dict(channel_rows_in=channel_rows_in, gate_rows_in=gate_rows_in, map_input_rows=map_input_rows, step_size_input=step_size_input, channel_kernel_weight=channel_kernel_weight, map_kernel_weight=map_kernel_weight, channel_conv_bias=channel_conv_bias, map_kernel_bias=map_kernel_bias, step_size_bias=step_size_bias, head_decay_rate=head_decay_rate, head_skip_weight=head_skip_weight, gated_norm_scale=gated_norm_scale, scan_state_cache=scan_state_cache, channel_window_cache=channel_window_cache, map_window_cache=map_window_cache, adapter_down_weight=adapter_down_weight, adapter_up_weight=adapter_up_weight, session_slot_index=session_slot_index, lengths=lengths, session_adapter_index=session_adapter_index)


NORM_EPS = 1e-05

def sigmoid_linear(value):
    return value / (1.0 + jnp.exp(-value))

def conv_part(cached, fresh, weight, offset):
    extended = jnp.concatenate([cached.astype(jnp.float32), fresh.astype(jnp.float32)], axis=1)
    span_len = fresh.shape[1]
    summed = offset + weight[0] * extended[:, 0:span_len] + weight[1] * extended[:, 1:span_len + 1]
    summed = summed + weight[2] * extended[:, 2:span_len + 2] + weight[3] * extended[:, 3:span_len + 3]
    return (sigmoid_linear(summed), extended)

def tail_state(extended, lengths):
    picked = lengths[:, None] + jnp.arange(3, dtype=jnp.int32)[None, :]
    picked = jnp.broadcast_to(picked[:, :, None], (extended.shape[0], 3, extended.shape[2]))
    return jnp.take_along_axis(extended, picked, axis=1).astype(jnp.bfloat16)

def scan_session(x_heads, map_rows, step_size, state_old, head_decay_rate, head_skip_weight):
    highest = lax.Precision.HIGHEST
    state_dim = map_rows.shape[1] // 2
    input_map = map_rows[:, :state_dim]
    output_map = map_rows[:, state_dim:]
    log_decay = jnp.cumsum(-head_decay_rate[:, None] * step_size, axis=1)
    span_len = step_size.shape[1]
    causal_mask = jnp.arange(span_len)[:, None] >= jnp.arange(span_len)[None, :]
    spread = log_decay[:, :, None] - log_decay[:, None, :]
    decay_mat = jnp.where(causal_mask[None], jnp.exp(jnp.where(causal_mask[None], spread, 0.0)), 0.0)
    scores = jnp.dot(output_map, input_map.T, precision=highest)
    scaled_x = x_heads * jnp.transpose(step_size)[:, :, None]
    inside = jnp.einsum('htu,uhp->thp', decay_mat * scores[None], scaled_x, precision=highest)
    carried = jnp.einsum('tn,hpn->thp', output_map, state_old, precision=highest)
    carried = carried * jnp.exp(jnp.transpose(log_decay))[:, :, None]
    mixed_out = inside + carried + head_skip_weight[None, :, None] * x_heads
    final_log = log_decay[:, -1]
    weights = jnp.exp(final_log[:, None] - log_decay) * step_size
    state_new = jnp.exp(final_log)[:, None, None] * state_old
    state_new = state_new + jnp.einsum('ht,thp,tn->hpn', weights, x_heads, input_map, precision=highest)
    return (mixed_out, state_new)

def reference(channel_rows_in, gate_rows_in, map_input_rows, step_size_input, channel_kernel_weight, map_kernel_weight, channel_conv_bias, map_kernel_bias, step_size_bias, head_decay_rate, head_skip_weight, gated_norm_scale, scan_state_cache, channel_window_cache, map_window_cache, adapter_down_weight, adapter_up_weight, session_slot_index, lengths, session_adapter_index):
    session_total, span_len, channels = channel_rows_in.shape
    head_count = head_decay_rate.shape[0]
    head_dim = channels // head_count
    conv_x, ext_x = conv_part(channel_window_cache[session_slot_index], channel_rows_in, channel_kernel_weight, channel_conv_bias)
    conv_m, ext_m = conv_part(map_window_cache[session_slot_index], map_input_rows, map_kernel_weight, map_kernel_bias)
    valid = (jnp.arange(span_len, dtype=jnp.int32)[None, :] < lengths[:, None]).astype(jnp.float32)
    step_size = jax.nn.softplus(step_size_input.astype(jnp.float32) + step_size_bias[None, :, None]) * valid[:, None, :]

    def one_session(operands):
        x_one, map_one, step_one, state_one = operands
        return scan_session(x_one.reshape(span_len, head_count, head_dim), map_one, step_one, state_one.astype(jnp.float32), head_decay_rate, head_skip_weight)
    mixed, state_new = lax.map(one_session, (conv_x, conv_m, step_size, scan_state_cache[session_slot_index]))
    mixed = mixed.reshape(session_total, span_len, channels) * valid[:, :, None]
    gated = mixed * sigmoid_linear(gate_rows_in.astype(jnp.float32))
    inv_rms = lax.rsqrt(lax.optimization_barrier(jnp.mean(gated * gated, axis=2)) + NORM_EPS)
    mixer_output_rows = (gated * inv_rms[:, :, None] * gated_norm_scale).astype(jnp.bfloat16)

    def adapter_apply(operands):
        scan_output_rows, adapter_choice = operands
        low_rank_rows = jnp.dot(scan_output_rows, adapter_down_weight[adapter_choice].T, preferred_element_type=jnp.float32).astype(jnp.bfloat16)
        return jnp.dot(low_rank_rows, adapter_up_weight[adapter_choice], preferred_element_type=jnp.float32).astype(jnp.bfloat16)
    adapter_delta = lax.map(adapter_apply, (mixer_output_rows, session_adapter_index))
    scan_state_next = jnp.zeros(scan_state_cache.shape, jnp.bfloat16).at[session_slot_index].set(state_new.astype(jnp.bfloat16))
    channel_window_next = jnp.zeros(channel_window_cache.shape, jnp.bfloat16).at[session_slot_index].set(tail_state(ext_x, lengths))
    map_window_next = jnp.zeros(map_window_cache.shape, jnp.bfloat16).at[session_slot_index].set(tail_state(ext_m, lengths))
    return (mixer_output_rows, adapter_delta, scan_state_next, channel_window_next, map_window_next)
```

```python
import jax
import jax.numpy as jnp
from jax import lax
from jax.experimental import pallas as pl
from jax.experimental.pallas import tpu as pltpu
from jax.sharding import PartitionSpec as P


NORM_EPS = 1e-05
PAIR = 2
CHUNKS = 2
GROUP = 4
BATCH = 4

F32 = jnp.float32
BF16 = jnp.bfloat16


def silu(value):
    return value / (1.0 + jnp.exp(-value))


def halves(value):
    high = value.astype(BF16)
    return high, (value - high.astype(F32)).astype(BF16)


def dot_nn(left, right):
    return lax.dot_general(left, right, (((1,), (0,)), ((), ())), preferred_element_type=F32)


def dot_nt(left, right):
    return lax.dot_general(left, right, (((1,), (1,)), ((), ())), preferred_element_type=F32)


def dot_tn(left, right):
    return lax.dot_general(left, right, (((0,), (0,)), ((), ())), preferred_element_type=F32)


def params(megabytes=62):
    return pltpu.CompilerParams(vmem_limit_bytes=megabytes * 1024 * 1024)


def cost(flops, moved, transcendentals=0):
    return pl.CostEstimate(
        flops=int(flops), bytes_accessed=int(moved), transcendentals=int(transcendentals)
    )


def convolve(ext_ref, kernel_rows, offset, tokens):
    summed = offset + kernel_rows[0:1] * ext_ref[5 : 5 + tokens]
    for tap in range(1, 4):
        summed = summed + kernel_rows[tap : tap + 1] * ext_ref[5 + tap : 5 + tap + tokens]
    return silu(summed)


def pack_small(slots, rank_here, map_slice, step_rows):
    sessions, group_tokens, width = map_slice.shape
    rows = lax.axis_size("row")

    def body(slot_ref, rank_ref, map_ref, step_ref, out_ref, held_ref):
        for q in range(sessions):
            slot = slot_ref[q]
            home = slot // PAIR
            rank = slot % PAIR
            held_ref[home, pl.ds(rank, 1), :] = step_ref[q : q + 1, :]

            @pl.when(rank == rank_ref[0])
            def _():
                out_ref[home, 0:group_tokens, :] = map_ref[q]

        out_ref[:, group_tokens:, :] = held_ref[...].astype(BF16)

    vmem = pl.BlockSpec(memory_space=pltpu.VMEM)
    smem = pl.BlockSpec(memory_space=pltpu.SMEM)
    return pl.pallas_call(
        body,
        out_shape=jax.ShapeDtypeStruct((rows, group_tokens + 8, width), BF16),
        in_specs=[smem, smem, vmem, vmem],
        out_specs=vmem,
        scratch_shapes=[pltpu.VMEM((rows, 8, width), F32)],
        compiler_params=params(),
        cost_estimate=cost(0, 1 << 20),
        name="pack_small",
    )(slots, rank_here, map_slice, step_rows)


def pack_channels(slots, rows_in, slot_total):
    sessions, tokens, channels = rows_in.shape
    width = channels // CHUNKS

    def body(slot_ref, in_ref, *rest):
        outs = rest[:CHUNKS]
        sems = rest[CHUNKS]

        def copies(q):
            slot = slot_ref[q]
            return [
                pltpu.make_async_copy(
                    in_ref.at[q, :, k * width : (k + 1) * width],
                    outs[k].at[slot],
                    sems.at[k * sessions + q],
                )
                for k in range(CHUNKS)
            ]

        for q in range(sessions):
            for copy in copies(q):
                copy.start()
        for q in range(sessions):
            for copy in copies(q):
                copy.wait()

    return pl.pallas_call(
        body,
        out_shape=[jax.ShapeDtypeStruct((slot_total, tokens, width), BF16)] * CHUNKS,
        in_specs=[
            pl.BlockSpec(memory_space=pltpu.SMEM),
            pl.BlockSpec(memory_space=pltpu.VMEM),
        ],
        out_specs=[pl.BlockSpec(memory_space=pl.ANY)] * CHUNKS,
        scratch_shapes=[pltpu.SemaphoreType.DMA((CHUNKS * sessions,))],
        compiler_params=params(),
        cost_estimate=cost(0, 4 << 20),
        name="pack_channels",
    )(slots, rows_in)


def prepare(slots, lens, lens_col, maps, small, map_window, state, map_kernel, map_bias, bias_row, decay_row):
    sessions, heads, head_dim, state_dim = state.shape
    groups, rows, group_tokens, width = maps.shape
    side = groups // PAIR
    tokens = side * group_tokens
    spread = heads * tokens
    channels = heads * head_dim
    chunk_heads = heads // CHUNKS
    chunk_spread = chunk_heads * tokens
    maps = maps.reshape(PAIR, side, rows, group_tokens, width)
    same = (jnp.arange(spread)[:, None] // tokens == jnp.arange(spread)[None, :] // tokens).astype(BF16)
    wide = (jnp.arange(spread)[:, None] // tokens == jnp.arange(channels)[None, :] // head_dim).astype(BF16)

    def body(
        slot_ref, len_ref, col_ref, *refs
    ):
        map_refs = refs[:BATCH]
        (
            small_ref, win_ref, state_ref, kern_ref, off_ref, bias_ref, rate_ref, same_ref, wide_ref,
            mat_ref, part_ref, wx_ref, in_ref, last_ref, tail_ref, raw_sc, step_sc, log_sc, weight_sc,
        ) = refs[BATCH : BATCH + 19]
        exts = refs[BATCH + 19 :]
        lane = lax.broadcasted_iota(jnp.int32, (1, spread), 1) % tokens

        @pl.when(pl.program_id(0) == 0)
        def _():
            for s in range(sessions):
                slot = slot_ref[s]
                pair = small_ref[slot // PAIR].astype(F32)
                raw_sc[s : s + 1, :] = jnp.where(slot % PAIR == 0, pair[0:1], pair[1:2])
            valid = (lane < col_ref[...]).astype(F32)
            step = jax.nn.softplus(raw_sc[...] + bias_ref[...]) * valid
            fall = -rate_ref[...] * step
            log = fall
            rest = jnp.where(lane < tokens - 1, pltpu.roll(fall, spread - 1, 1), 0.0)
            hop = 1
            while hop < tokens:
                log = log + jnp.where(lane >= hop, pltpu.roll(log, hop, 1), 0.0)
                rest = rest + jnp.where(lane < tokens - hop, pltpu.roll(rest, spread - hop, 1), 0.0)
                hop *= 2
            step_sc[...] = step
            log_sc[...] = log
            weight_sc[...] = jnp.exp(rest) * step

        token = lax.broadcasted_iota(jnp.int32, (tokens, spread), 0)
        within = lax.broadcasted_iota(jnp.int32, (tokens, spread), 1) % tokens
        diagonal = within == token
        causal = within <= token
        final = lax.broadcasted_iota(jnp.int32, (heads, spread), 1) == (
            lax.broadcasted_iota(jnp.int32, (heads, spread), 0) * tokens + tokens - 1
        )
        for i in range(BATCH):
            c = pl.program_id(0) * BATCH + i
            ext_sc = exts[i]
            step = step_sc[pl.ds(c, 1), :]
            log = log_sc[pl.ds(c, 1), :]
            weight = weight_sc[pl.ds(c, 1), :]
            ext_sc[5:8] = win_ref[i].astype(F32)
            ext_sc[8:] = map_refs[i][0, :, 0].astype(F32).reshape(tokens, width)
            tail_ref[i] = jnp.concatenate(
                [ext_sc[pl.ds(len_ref[c] + 5 + n, 1), :] for n in range(3)], axis=0
            ).astype(BF16)
            conv = convolve(ext_sc, kern_ref[...], off_ref[...], tokens)
            in_high, in_low = halves(conv[:, :state_dim])
            out_high, out_low = halves(conv[:, state_dim:])
            in_ref[i] = jnp.concatenate([in_high, in_low, in_high], axis=0)

            log_all = jnp.broadcast_to(log, (tokens, spread))
            spot = jnp.where(diagonal, log_all, 0.0)
            first = spot.astype(BF16)
            second, third = halves(spot - first.astype(F32))
            own = dot_nn(jnp.concatenate([first, second, third], axis=0), same_ref[...])
            own = own[:tokens] + own[tokens : 2 * tokens] + own[2 * tokens :]
            decay = jnp.where(causal, jnp.exp(jnp.where(causal, own - log_all, 0.0)), 0.0)
            keys = jnp.concatenate([jnp.concatenate([in_high, in_low], axis=1)] * heads, axis=0)
            asks = jnp.concatenate(
                [
                    jnp.concatenate([out_high, out_high], axis=1),
                    jnp.concatenate([out_low, jnp.zeros_like(out_low)], axis=1),
                ],
                axis=0,
            )
            scores = dot_nt(asks, keys)
            scores = scores[:tokens] + scores[tokens:]
            high, low = halves(decay * scores * step)
            for k in range(CHUNKS):
                part = slice(k * chunk_spread, (k + 1) * chunk_spread)
                base = 2 * k * chunk_spread
                mat_ref[i, :, base : base + chunk_spread] = high[:, part]
                mat_ref[i, :, base + chunk_spread : base + 2 * chunk_spread] = low[:, part]

            rise = halves(jnp.where(diagonal, jnp.exp(log_all), 0.0))
            load = halves(jnp.where(diagonal, jnp.broadcast_to(weight, (tokens, spread)), 0.0))
            grown = dot_nn(jnp.concatenate([*rise, *load], axis=0), wide_ref[...])
            wx_ref[i] = grown[2 * tokens : 3 * tokens] + grown[3 * tokens :]
            carried = dot_nt(
                jnp.concatenate([out_high, out_low], axis=0), state_ref[i].reshape(channels, state_dim)
            )
            part_ref[i] = (carried[:tokens] + carried[tokens:]) * (
                grown[:tokens] + grown[tokens : 2 * tokens]
            )
            last = jnp.sum(jnp.where(final, jnp.exp(log), 0.0), axis=1, keepdims=True)
            last_ref[i] = jnp.broadcast_to(last, (heads, 128))

    def whole(*shape):
        return pl.BlockSpec(shape, lambda g, s, n: (0,) * len(shape))

    def at(*shape):
        return pl.BlockSpec((BATCH,) + shape, lambda g, s, n: (g,) + (0,) * len(shape))

    def received(i):
        return pl.BlockSpec(
            (1, side, 1, group_tokens, width),
            lambda g, s, n: (s[g * BATCH + i] % PAIR, 0, s[g * BATCH + i] // PAIR, 0, 0),
        )

    return pl.pallas_call(
        body,
        out_shape=[
            jax.ShapeDtypeStruct((sessions, tokens, 2 * spread), BF16),
            jax.ShapeDtypeStruct((sessions, tokens, channels), F32),
            jax.ShapeDtypeStruct((sessions, tokens, channels), F32),
            jax.ShapeDtypeStruct((sessions, 3 * tokens, state_dim), BF16),
            jax.ShapeDtypeStruct((sessions, heads, 128), F32),
            jax.ShapeDtypeStruct((sessions, 3, width), BF16),
        ],
        grid_spec=pltpu.PrefetchScalarGridSpec(
            num_scalar_prefetch=2,
            grid=(sessions // BATCH,),
            in_specs=[whole(sessions, 1)]
            + [received(i) for i in range(BATCH)]
            + [
                pl.BlockSpec((rows, 8, width), lambda g, s, n: (0, group_tokens // 8, 0)),
                at(3, width),
                at(heads, head_dim, state_dim),
                whole(4, width),
                whole(1, width),
                whole(1, spread),
                whole(1, spread),
                whole(spread, spread),
                whole(spread, channels),
            ],
            out_specs=[
                at(tokens, 2 * spread),
                at(tokens, channels),
                at(tokens, channels),
                at(3 * tokens, state_dim),
                at(heads, 128),
                at(3, width),
            ],
            scratch_shapes=[pltpu.VMEM((sessions, spread), F32)] * 4
            + [pltpu.VMEM((tokens + 8, width), F32)] * BATCH,
        ),
        compiler_params=params(),
        cost_estimate=cost(sessions * (1 << 25), sessions << 19),
        name="prepare",
    )(
        slots, lens, lens_col, *[maps] * BATCH, small, map_window, state, map_kernel, map_bias, bias_row,
        decay_row, same, wide,
    )


def mix(k, slots, lens, fresh, window, prepared, state, kernel, offset, skip, earlier):
    mats, parts, loads, in_maps, lasts = prepared
    slot_total, tokens, width = fresh.shape
    sessions, heads, head_dim, state_dim = state.shape
    chunk_heads = heads // CHUNKS
    chunk_spread = chunk_heads * tokens
    channels = heads * head_dim

    def body(slot_ref, len_ref, *refs):
        new_refs = refs[:BATCH]
        (
            win_ref, mat_ref, part_ref, wx_ref, in_ref, last_ref, state_ref, kern_ref, off_ref, skip_ref,
        ) = refs[BATCH : BATCH + 10]
        y_ref, next_ref, tail_ref, y_sc, sems, *exts = refs[BATCH + 10 + len(earlier) :]
        g = pl.program_id(0)
        turn = g % 2

        def copy(i, group, half):
            return pltpu.make_async_copy(
                y_sc.at[half, i], y_ref.at[slot_ref[group * BATCH + i]], sems.at[half, i]
            )

        @pl.when(g >= 2)
        def _():
            for i in range(BATCH):
                copy(i, g - 2, turn).wait()

        owner = lax.broadcasted_iota(jnp.int32, (chunk_spread, width), 0) // tokens
        lane = lax.broadcasted_iota(jnp.int32, (chunk_spread, width), 1) // head_dim
        own = owner == lane
        zero = jnp.zeros((chunk_spread, width), BF16)
        token = lax.broadcasted_iota(jnp.int32, (tokens, width), 0)
        for i in range(BATCH):
            c = g * BATCH + i
            ext_sc = exts[i]
            ext_sc[5:8] = win_ref[i].astype(F32)
            ext_sc[8:] = new_refs[i][0].astype(F32)
            tail_ref[i] = jnp.concatenate(
                [ext_sc[pl.ds(len_ref[c] + 5 + n, 1), :] for n in range(3)], axis=0
            ).astype(BF16)
            x = convolve(ext_sc, kern_ref[...], off_ref[...], tokens)
            high, low = halves(x)
            tall_high = jnp.where(own, jnp.concatenate([high] * chunk_heads, axis=0), zero)
            tall_low = jnp.where(own, jnp.concatenate([low] * chunk_heads, axis=0), zero)
            mat = mat_ref[i]
            inside = dot_nn(
                jnp.concatenate([mat, mat[:, :chunk_spread]], axis=1),
                jnp.concatenate([tall_high, tall_high, tall_low], axis=0),
            )
            mixed = inside + part_ref[i] + skip_ref[...] * x
            y_sc[turn, i] = jnp.where(token < len_ref[c], mixed, 0.0).astype(BF16)
            copy(i, g, turn).start()
            w_high, w_low = halves(x * wx_ref[i])
            added = dot_tn(jnp.concatenate([w_high, w_high, w_low], axis=0), in_ref[i])
            for h in range(chunk_heads):
                at = k * chunk_heads + h
                next_ref[i, h] = (
                    last_ref[i, at : at + 1, :] * state_ref[i, h].astype(F32)
                    + added[h * head_dim : (h + 1) * head_dim]
                ).astype(BF16)

        @pl.when(g == pl.num_programs(0) - 1)
        def _():
            for i in range(BATCH):
                copy(i, g - 1, 1 - turn).wait()
                copy(i, g, turn).wait()

    def whole(*shape):
        return pl.BlockSpec(shape, lambda g, s, n: (0,) * (len(shape) - 1) + (k,))

    def cut(*shape):
        return pl.BlockSpec((BATCH,) + shape, lambda g, s, n: (g,) + (0,) * (len(shape) - 1) + (k,))

    def at(*shape):
        return pl.BlockSpec((BATCH,) + shape, lambda g, s, n: (g,) + (0,) * len(shape))

    def received(i):
        return pl.BlockSpec((1, tokens, width), lambda g, s, n: (s[g * BATCH + i], 0, 0))

    held = pl.BlockSpec((BATCH, chunk_heads, head_dim, state_dim), lambda g, s, n: (g, k, 0, 0))
    anywhere = pl.BlockSpec(memory_space=pl.ANY)
    operands = [slots, lens, *[fresh] * BATCH, window, mats, parts, loads, in_maps, lasts]
    operands += [state, kernel, offset, skip]
    return pl.pallas_call(
        body,
        out_shape=[
            jax.ShapeDtypeStruct((slot_total, tokens, width), BF16),
            jax.ShapeDtypeStruct(state.shape, BF16),
            jax.ShapeDtypeStruct((sessions, 3, channels), BF16),
        ],
        grid_spec=pltpu.PrefetchScalarGridSpec(
            num_scalar_prefetch=2,
            grid=(sessions // BATCH,),
            in_specs=[received(i) for i in range(BATCH)]
            + [
                cut(3, width),
                cut(tokens, 2 * chunk_spread),
                cut(tokens, width),
                cut(tokens, width),
                at(3 * tokens, state_dim),
                at(heads, 128),
                held,
                whole(4, width),
                whole(1, width),
                whole(1, width),
            ]
            + [anywhere] * len(earlier),
            out_specs=[anywhere, held, cut(3, width)],
            scratch_shapes=[
                pltpu.VMEM((2, BATCH, tokens, width), BF16),
                pltpu.SemaphoreType.DMA((2, BATCH)),
            ]
            + [pltpu.VMEM((tokens + 8, width), F32)] * BATCH,
        ),
        input_output_aliases={len(operands) + i: 1 + i for i in range(len(earlier))},
        compiler_params=params(),
        cost_estimate=cost(sessions * (1 << 24), sessions << 19),
    )(*operands, *earlier)


def gate_rows(k, slots, picks, back, gate, adapters, scale, earlier):
    sessions, tokens, _ = gate.shape
    _, _, width = back.shape
    rank = adapters.shape[1] // 2

    def body(slot_ref, pick_ref, *refs):
        backs, downs = refs[:GROUP], refs[GROUP : 2 * GROUP]
        gate_ref, scale_ref = refs[2 * GROUP : 2 * GROUP + 2]
        sum_ref, gated_ref = refs[-2:]
        for i in range(GROUP):
            gated = backs[i][0].astype(F32) * silu(gate_ref[i].astype(F32))
            gated_ref[i] = gated
            low = dot_nt((gated * scale_ref[...]).astype(BF16), downs[i][0])
            square = jnp.sum(gated * gated, axis=1, keepdims=True)
            both = jnp.concatenate([low, jnp.broadcast_to(square, (tokens, 128 - rank))], axis=1)
            if earlier:
                both = both + refs[2 * GROUP + 2][i * tokens : (i + 1) * tokens]
            sum_ref[i * tokens : (i + 1) * tokens] = both

    def returned(i):
        return pl.BlockSpec((1, tokens, width), lambda g, s, a: (s[g * GROUP + i], 0, 0))

    def chosen(i):
        return pl.BlockSpec((1, rank, width), lambda g, s, a: (a[g * GROUP + i], 0, k))

    sums = pl.BlockSpec((GROUP * tokens, 128), lambda g, s, a: (g, 0))
    return pl.pallas_call(
        body,
        out_shape=[
            jax.ShapeDtypeStruct((sessions * tokens, 128), F32),
            jax.ShapeDtypeStruct((sessions, tokens, width), F32),
        ],
        grid_spec=pltpu.PrefetchScalarGridSpec(
            num_scalar_prefetch=2,
            grid=(sessions // GROUP,),
            in_specs=[returned(i) for i in range(GROUP)]
            + [chosen(i) for i in range(GROUP)]
            + [
                pl.BlockSpec((GROUP, tokens, width), lambda g, s, a: (g, 0, k)),
                pl.BlockSpec((1, width), lambda g, s, a: (0, k)),
            ]
            + [sums] * len(earlier),
            out_specs=[sums, pl.BlockSpec((GROUP, tokens, width), lambda g, s, a: (g, 0, 0))],
        ),
        compiler_params=params(),
        cost_estimate=cost(sessions * (1 << 22), sessions << 18),
    )(slots, picks, *[back] * GROUP, *[adapters] * GROUP, gate, scale, *earlier)


def finish(picks, gated, totals, adapters, scale):
    sessions, tokens, width = gated[0].shape
    channels = width * CHUNKS
    rank = adapters.shape[1] // 2

    def body(pick_ref, *refs):
        ups, rows = refs[:GROUP], refs[GROUP : GROUP + CHUNKS]
        total_ref, scale_ref, out_ref, delta_ref = refs[GROUP + CHUNKS :]
        for i in range(GROUP):
            total = total_ref[i * tokens : (i + 1) * tokens]
            inverse = total[:, rank : rank + 1]
            for k in range(CHUNKS):
                part = slice(k * width, (k + 1) * width)
                out_ref[i, :, part] = (rows[k][i] * inverse * scale_ref[:, part]).astype(BF16)
            delta_ref[i] = dot_nn(total[:, :rank].astype(BF16), ups[i][0]).astype(BF16)

    def chosen(i):
        return pl.BlockSpec((1, rank, channels), lambda g, a: (a[g * GROUP + i], 1, 0))

    out = pl.BlockSpec((GROUP, tokens, channels), lambda g, a: (g, 0, 0))
    return pl.pallas_call(
        body,
        out_shape=[jax.ShapeDtypeStruct((sessions, tokens, channels), BF16)] * 2,
        grid_spec=pltpu.PrefetchScalarGridSpec(
            num_scalar_prefetch=1,
            grid=(sessions // GROUP,),
            in_specs=[chosen(i) for i in range(GROUP)]
            + [pl.BlockSpec((GROUP, tokens, width), lambda g, a: (g, 0, 0))] * CHUNKS
            + [
                pl.BlockSpec((GROUP * tokens, 128), lambda g, a: (g, 0)),
                pl.BlockSpec((1, channels), lambda g, a: (0, 0)),
            ],
            out_specs=[out, out],
        ),
        compiler_params=params(),
        cost_estimate=cost(sessions * (1 << 22), sessions << 18),
        name="finish",
    )(picks, *[adapters] * GROUP, *gated, totals, scale)


def exchange(value, axis, groups=None):
    return lax.all_to_all(
        value, axis, split_axis=0, concat_axis=0, tiled=True, axis_index_groups=groups
    )


def share_all(value, axis, count, groups=None):
    return exchange(
        jnp.broadcast_to(value[None], (count,) + value.shape).reshape((-1,) + value.shape[1:]), axis, groups
    )


def place(spots, blocks):
    count = len(blocks)

    def body(spot_ref, *refs):
        ins, out_ref = refs[:count], refs[count]
        helds, sems = refs[count + 1 : 2 * count + 1], refs[2 * count + 1]
        loads = [pltpu.make_async_copy(ins[i], helds[i], sems.at[0, i]) for i in range(count)]
        for load in loads:
            load.start()
        stores = []
        for i in range(count):
            loads[i].wait()
            stores.append(pltpu.make_async_copy(helds[i], out_ref.at[spot_ref[i]], sems.at[1, i]))
            stores[i].start()
        for store in stores:
            store.wait()

    return pl.pallas_call(
        body,
        out_shape=jax.ShapeDtypeStruct((count,) + blocks[0].shape, blocks[0].dtype),
        in_specs=[pl.BlockSpec(memory_space=pltpu.SMEM)]
        + [pl.BlockSpec(memory_space=pl.ANY)] * count,
        out_specs=pl.BlockSpec(memory_space=pl.ANY),
        scratch_shapes=[pltpu.VMEM(block.shape, block.dtype) for block in blocks]
        + [pltpu.SemaphoreType.DMA((2, count))],
        compiler_params=params(),
        cost_estimate=cost(0, 2 * count * blocks[0].size * 2),
    )(spots, *blocks)


def shifted(value, axis, rings):
    length = len(rings[0])
    held = [value]
    for d in range(1, length):
        pairs = [(ring[i], ring[(i + d) % length]) for ring in rings for i in range(length)]
        held.append(lax.ppermute(value, axis, pairs))
    return held


def origins(position, length):
    return (position - jnp.arange(length, dtype=jnp.int32)) % length


def gather_adapters(block, row, size_z, size_x):
    along_z = [[z * size_x + x for z in range(size_z)] for x in range(size_x)]
    along_x = [[z * size_x + x for x in range(size_x)] for z in range(size_z)]
    column = place(origins(row // size_x, size_z), shifted(block, "row", along_z))
    whole = place(origins(row % size_x, size_x), shifted(column, "row", along_x))
    return whole.reshape((size_z * size_x,) + block.shape)


def shards(
    channel_rows_in,
    gate_rows_in,
    map_input_rows,
    step_size_input,
    channel_kernel_weight,
    map_kernel_weight,
    channel_conv_bias,
    map_kernel_bias,
    step_size_bias,
    head_decay_rate,
    head_skip_weight,
    gated_norm_scale,
    scan_state_cache,
    channel_window_cache,
    map_window_cache,
    adapter_down_weight,
    adapter_up_weight,
    session_slot_index,
    lengths,
    session_adapter_index,
):
    sessions, tokens, channels = channel_rows_in.shape
    heads = step_size_input.shape[1]
    head_dim = channels // heads
    rows = lax.axis_size("row")
    sections = lax.axis_size("section")
    row = lax.axis_index("row")
    section = lax.axis_index("section")
    size_x = 4 if rows >= 32 else 2
    size_z = rows // size_x
    side = sections // PAIR
    group_tokens = tokens // side

    local = jnp.arange(sessions, dtype=jnp.int32)
    mine = lax.dynamic_slice_in_dim(session_slot_index, row * sessions, sessions)
    homes = mine // sessions
    sooner = (homes[None, :] == homes[:, None]) & (local[None, :] < local[:, None])
    serve_slots = homes * PAIR + jnp.sum(sooner.astype(jnp.int32), axis=1)
    here = (session_slot_index // sessions == row).astype(jnp.int32).reshape(rows, sessions)
    ahead = jnp.sum(
        jnp.where(local[None, None, :] < local[None, :, None], here[:, None, :], 0), axis=2
    )
    target = (jnp.arange(rows, dtype=jnp.int32)[:, None] * PAIR + ahead).reshape(-1)
    match = session_slot_index[None, :] == (row * sessions + local)[:, None]
    home_slots = jnp.sum(jnp.where(match, target[None, :], 0), axis=1)
    home_lens = jnp.sum(jnp.where(match, lengths[None, :], 0), axis=1)
    adapter = lax.dynamic_slice_in_dim(session_adapter_index, row * sessions, sessions)
    picks = adapter % size_x * size_z + adapter // size_x

    map_slice = lax.dynamic_slice_in_dim(
        map_input_rows, section % side * group_tokens, group_tokens, axis=1
    )
    step_rows = step_size_input.reshape(sessions, heads * tokens).astype(F32)
    small = pack_small(serve_slots, (section // side).reshape(1), map_slice, step_rows)
    small = exchange(small, "row")
    sent = pack_channels(serve_slots, channel_rows_in, rows * PAIR)
    fresh = []
    for k in range(CHUNKS):
        fresh.append(exchange(sent[k], "row"))
    block = jnp.concatenate([adapter_down_weight[0], adapter_up_weight[0]], axis=0)
    adapters = gather_adapters(block, row, size_z, size_x)
    maps = place(
        origins(section, sections),
        shifted(small[:, :group_tokens], "section", [list(range(sections))]),
    )
    *prepared, map_window_next = prepare(
        home_slots,
        home_lens,
        home_lens[:, None],
        maps,
        small,
        map_window_cache,
        scan_state_cache,
        map_kernel_weight,
        map_kernel_bias[None],
        jnp.repeat(step_size_bias, tokens)[None],
        jnp.repeat(head_decay_rate, tokens)[None],
    )
    skip = jnp.repeat(head_skip_weight, head_dim)[None]
    scale = gated_norm_scale[None]
    back = []
    carried = []
    for k in range(CHUNKS):
        mixed, *carried = mix(
            k,
            home_slots,
            home_lens,
            fresh[k],
            channel_window_cache,
            prepared,
            scan_state_cache,
            channel_kernel_weight,
            channel_conv_bias[None],
            skip,
            carried,
        )
        back.append(exchange(mixed, "row"))
    scan_state_next, channel_window_next = carried
    sums = []
    gated = []
    for k in range(CHUNKS):
        total, part = gate_rows(k, serve_slots, picks, back[k], gate_rows_in, adapters, scale, sums)
        sums = [total]
        gated.append(part)
    rank = adapter_down_weight.shape[1]
    share = exchange(sums[0], "section")
    share = jnp.sum(share.reshape(sections, -1, 128), axis=0)
    inverse = lax.rsqrt(share[:, rank:] / (channels * sections) + NORM_EPS)
    share = jnp.concatenate([share[:, :rank] * inverse[:, :1], inverse], axis=1)
    totals = share_all(share, "section", sections)
    mixer_output_rows, adapter_delta = finish(picks, gated, totals, adapters, scale)
    return (mixer_output_rows, adapter_delta, scan_state_next, channel_window_next, map_window_next)


def solution(mesh):
    split = P("row", None, "section")
    return jax.shard_map(
        shards,
        mesh=mesh,
        in_specs=(
            split,
            split,
            P("row", None, None),
            P("row", "section", None),
            P(None, "section"),
            P(),
            P("section"),
            P(),
            P("section"),
            P("section"),
            P("section"),
            P("section"),
            P("row", "section", None, None),
            split,
            P("row", None, None),
            split,
            split,
            P(),
            P(),
            P(),
        ),
        out_specs=(
            split,
            split,
            P("row", "section", None, None),
            split,
            P("row", None, None),
        ),
        check_vma=False,
    )
```

```python
import jax
import jax.numpy as jnp
from jax import lax
from jax.experimental import pallas as pl
from jax.experimental.pallas import tpu as pltpu
from jax.sharding import PartitionSpec as P


NORM_EPS = 1e-05
PAIR = 2
CHUNKS = 2
GROUP = 16
BATCH = 8

BLOCK = 4

F32 = jnp.float32
BF16 = jnp.bfloat16


def silu(value):
    return value / (1.0 + jnp.exp(-value))


def halves(value):
    high = value.astype(BF16)
    return high, (value - high.astype(F32)).astype(BF16)


def dot_nn(left, right):
    return lax.dot_general(left, right, (((1,), (0,)), ((), ())), preferred_element_type=F32)


def dot_nt(left, right):
    return lax.dot_general(left, right, (((1,), (1,)), ((), ())), preferred_element_type=F32)


def dot_tn(left, right):
    return lax.dot_general(left, right, (((0,), (0,)), ((), ())), preferred_element_type=F32)


def params(megabytes=62):
    return pltpu.CompilerParams(vmem_limit_bytes=megabytes * 1024 * 1024)


def cost(flops, moved, transcendentals=0):
    return pl.CostEstimate(
        flops=int(flops), bytes_accessed=int(moved), transcendentals=int(transcendentals)
    )


def convolve(ext_ref, kernel_rows, offset, tokens):
    summed = offset + kernel_rows[0:1] * ext_ref[5 : 5 + tokens]
    for tap in range(1, 4):
        summed = summed + kernel_rows[tap : tap + 1] * ext_ref[5 + tap : 5 + tap + tokens]
    return silu(summed)


def pack(slots, rank_here, map_slice, step_rows, rows_in, slot_total):
    sessions, tokens, channels = rows_in.shape
    _, group_tokens, map_width = map_slice.shape
    width = channels // CHUNKS
    extra = max(group_tokens, 8)

    def body(slot_ref, rank_ref, map_ref, step_ref, in_ref, *rest):
        outs = rest[:CHUNKS]
        small_sc, step_sc, sems, small_sem = rest[CHUNKS:]

        def copies(q):
            slot = slot_ref[q]
            return [
                pltpu.make_async_copy(
                    in_ref.at[q, :, k * width : (k + 1) * width],
                    outs[k].at[slot, 0:tokens, :],
                    sems.at[k * sessions + q],
                )
                for k in range(CHUNKS)
            ]

        for q in range(sessions):
            for copy in copies(q):
                copy.start()
        for q in range(sessions):
            home = slot_ref[q] // PAIR
            rank = slot_ref[q] % PAIR
            step_sc[home, pl.ds(rank, 1), :] = step_ref[q : q + 1, :]

            @pl.when(rank == rank_ref[0])
            def _():
                small_sc[home, 0, 0:group_tokens] = map_ref[q]

        small_sc[:, 1, 0:8] = step_sc[...].astype(BF16)
        smalls = [
            pltpu.make_async_copy(
                small_sc.at[home], outs[0].at[pl.ds(home * PAIR, PAIR), tokens:, :], small_sem.at[home]
            )
            for home in range(slot_total // PAIR)
        ]
        for copy in smalls:
            copy.start()
        for q in range(sessions):
            for copy in copies(q):
                copy.wait()
        for copy in smalls:
            copy.wait()

    vmem = pl.BlockSpec(memory_space=pltpu.VMEM)
    smem = pl.BlockSpec(memory_space=pltpu.SMEM)
    return pl.pallas_call(
        body,
        out_shape=[
            jax.ShapeDtypeStruct((slot_total, tokens + (extra if k == 0 else 0), width), BF16)
            for k in range(CHUNKS)
        ],
        in_specs=[smem, smem, vmem, vmem, vmem],
        out_specs=[pl.BlockSpec(memory_space=pl.ANY)] * CHUNKS,
        scratch_shapes=[
            pltpu.VMEM((slot_total // PAIR, PAIR, extra, map_width), BF16),
            pltpu.VMEM((slot_total // PAIR, 8, map_width), F32),
            pltpu.SemaphoreType.DMA((CHUNKS * sessions,)),
            pltpu.SemaphoreType.DMA((slot_total // PAIR,)),
        ],
        compiler_params=params(),
        cost_estimate=cost(0, 4 << 20),
        name="pack",
    )(slots, rank_here, map_slice, step_rows, rows_in)


def prepare(slots, lens, maps, fresh, map_window, state, map_kernel, map_bias, bias, decay):
    sessions, heads, head_dim, state_dim = state.shape
    groups, rows, group_tokens, width = maps.shape
    side = groups // PAIR
    tokens = side * group_tokens
    spread = heads * tokens
    channels = heads * head_dim
    chunk_heads = heads // CHUNKS
    chunk_spread = chunk_heads * tokens
    maps = maps.reshape(PAIR, side, rows, group_tokens, width)

    def per_head(values, size):
        lane = lax.broadcasted_iota(jnp.int32, (1, heads * size), 1) // size
        row = jnp.zeros((1, heads * size), F32)
        for h in range(heads):
            row = jnp.where(lane == h, values[h], row)
        return row

    def blocks(columns, size):
        row = lax.broadcasted_iota(jnp.int32, (spread, columns), 0) // tokens
        column = lax.broadcasted_iota(jnp.int32, (spread, columns), 1) // size
        return jnp.where(row == column, 1.0, 0.0).astype(BF16)

    def body(slot_ref, len_ref, *refs):
        map_refs = refs[:BATCH]
        (
            small_ref, win_ref, state_ref, kern_ref, off_ref, bias_ref, rate_ref,
            mat_ref, part_ref, wx_ref, in_ref, last_ref, tail_ref,
            raw_sc, valid_sc, step_sc, log_sc, weight_sc, same_ref, wide_ref,
        ) = refs[BATCH : BATCH + 20]
        exts = refs[BATCH + 20 :]
        lane = lax.broadcasted_iota(jnp.int32, (1, spread), 1) % tokens

        @pl.when(pl.program_id(0) == 0)
        def _():
            same_ref[...] = blocks(spread, tokens)
            wide_ref[...] = blocks(channels, head_dim)
            for s in range(sessions):
                slot = slot_ref[s]
                pair = small_ref[slot // PAIR * PAIR + 1].astype(F32)
                raw_sc[s : s + 1, :] = jnp.where(slot % PAIR == 0, pair[0:1], pair[1:2])
                valid_sc[s : s + 1, :] = jnp.where(lane < len_ref[s], 1.0, 0.0)
            step = jax.nn.softplus(raw_sc[...] + per_head(bias_ref, tokens)) * valid_sc[...]
            fall = -per_head(rate_ref, tokens) * step
            log = fall
            rest = jnp.where(lane < tokens - 1, pltpu.roll(fall, spread - 1, 1), 0.0)
            hop = 1
            while hop < tokens:
                log = log + jnp.where(lane >= hop, pltpu.roll(log, hop, 1), 0.0)
                rest = rest + jnp.where(lane < tokens - hop, pltpu.roll(rest, spread - hop, 1), 0.0)
                hop *= 2
            step_sc[...] = step
            log_sc[...] = log
            weight_sc[...] = jnp.exp(rest) * step

        token = lax.broadcasted_iota(jnp.int32, (tokens, spread), 0)
        within = lax.broadcasted_iota(jnp.int32, (tokens, spread), 1) % tokens
        diagonal = within == token
        causal = within <= token
        final = lax.broadcasted_iota(jnp.int32, (heads, spread), 1) == (
            lax.broadcasted_iota(jnp.int32, (heads, spread), 0) * tokens + tokens - 1
        )
        for i in range(BATCH):
            c = pl.program_id(0) * BATCH + i
            ext_sc = exts[i]
            step = step_sc[pl.ds(c, 1), :]
            log = log_sc[pl.ds(c, 1), :]
            weight = weight_sc[pl.ds(c, 1), :]
            ext_sc[5:8] = win_ref[i].astype(F32)
            ext_sc[8:] = map_refs[i][0, :, 0].astype(F32).reshape(tokens, width)
            tail_ref[i] = jnp.concatenate(
                [ext_sc[pl.ds(len_ref[c] + 5 + n, 1), :] for n in range(3)], axis=0
            ).astype(BF16)
            conv = convolve(ext_sc, kern_ref[...], off_ref[...], tokens)
            in_high, in_low = halves(conv[:, :state_dim])
            out_high, out_low = halves(conv[:, state_dim:])
            in_ref[i] = jnp.concatenate([in_high, in_low, in_high], axis=0)

            log_all = jnp.broadcast_to(log, (tokens, spread))
            spot = jnp.where(diagonal, log_all, 0.0)
            first = spot.astype(BF16)
            second, third = halves(spot - first.astype(F32))
            own = dot_nn(jnp.concatenate([first, second, third], axis=0), same_ref[...])
            own = own[:tokens] + own[tokens : 2 * tokens] + own[2 * tokens :]
            decay = jnp.where(causal, jnp.exp(jnp.where(causal, own - log_all, 0.0)), 0.0)
            keys = jnp.concatenate([jnp.concatenate([in_high, in_low], axis=1)] * heads, axis=0)
            asks = jnp.concatenate(
                [
                    jnp.concatenate([out_high, out_high], axis=1),
                    jnp.concatenate([out_low, jnp.zeros_like(out_low)], axis=1),
                ],
                axis=0,
            )
            scores = dot_nt(asks, keys)
            scores = scores[:tokens] + scores[tokens:]
            high, low = halves(decay * scores * step)
            for k in range(CHUNKS):
                part = slice(k * chunk_spread, (k + 1) * chunk_spread)
                base = 2 * k * chunk_spread
                mat_ref[i, :, base : base + chunk_spread] = high[:, part]
                mat_ref[i, :, base + chunk_spread : base + 2 * chunk_spread] = low[:, part]

            rise = halves(jnp.where(diagonal, jnp.exp(log_all), 0.0))
            load = halves(jnp.where(diagonal, jnp.broadcast_to(weight, (tokens, spread)), 0.0))
            grown = dot_nn(jnp.concatenate([*rise, *load], axis=0), wide_ref[...])
            wx_ref[i] = grown[2 * tokens : 3 * tokens] + grown[3 * tokens :]
            carried = dot_nt(
                jnp.concatenate([out_high, out_low], axis=0), state_ref[i].reshape(channels, state_dim)
            )
            part_ref[i] = (carried[:tokens] + carried[tokens:]) * (
                grown[:tokens] + grown[tokens : 2 * tokens]
            )
            last = jnp.sum(jnp.where(final, jnp.exp(log), 0.0), axis=1, keepdims=True)
            last_ref[i] = jnp.broadcast_to(last, (heads, 128))

    def whole(*shape):
        return pl.BlockSpec(shape, lambda g, s, n: (0,) * len(shape))

    def at(*shape):
        return pl.BlockSpec((BATCH,) + shape, lambda g, s, n: (g,) + (0,) * len(shape))

    def received(i):
        return pl.BlockSpec(
            (1, side, 1, group_tokens, width),
            lambda g, s, n: (s[g * BATCH + i] % PAIR, 0, s[g * BATCH + i] // PAIR, 0, 0),
        )

    return pl.pallas_call(
        body,
        out_shape=[
            jax.ShapeDtypeStruct((sessions, tokens, 2 * spread), BF16),
            jax.ShapeDtypeStruct((sessions, tokens, channels), F32),
            jax.ShapeDtypeStruct((sessions, tokens, channels), F32),
            jax.ShapeDtypeStruct((sessions, 3 * tokens, state_dim), BF16),
            jax.ShapeDtypeStruct((sessions, heads, 128), F32),
            jax.ShapeDtypeStruct((sessions, 3, width), BF16),
        ],
        grid_spec=pltpu.PrefetchScalarGridSpec(
            num_scalar_prefetch=2,
            grid=(sessions // BATCH,),
            in_specs=[received(i) for i in range(BATCH)]
            + [
                pl.BlockSpec((rows * PAIR, 8, width), lambda g, s, n: (0, tokens // 8, 0)),
                at(3, width),
                at(heads, head_dim, state_dim),
                whole(4, width),
                whole(1, width),
                pl.BlockSpec(memory_space=pltpu.SMEM),
                pl.BlockSpec(memory_space=pltpu.SMEM),
            ],
            out_specs=[
                at(tokens, 2 * spread),
                at(tokens, channels),
                at(tokens, channels),
                at(3 * tokens, state_dim),
                at(heads, 128),
                at(3, width),
            ],
            scratch_shapes=[pltpu.VMEM((sessions, spread), F32)] * 5
            + [pltpu.VMEM((spread, spread), BF16), pltpu.VMEM((spread, channels), BF16)]
            + [pltpu.VMEM((tokens + 8, width), F32)] * BATCH,
        ),
        compiler_params=params(),
        cost_estimate=cost(sessions * (1 << 25), sessions << 19),
        name="prepare",
    )(
        slots, lens, *[maps] * BATCH, fresh, map_window, state, map_kernel, map_bias, bias, decay
    )


def mix(k, slots, lens, fresh, window, prepared, state, kernel, offset, skip, earlier):
    mats, parts, loads, in_maps, lasts = prepared
    slot_total, _, width = fresh.shape
    tokens = mats.shape[1]
    sessions, heads, head_dim, state_dim = state.shape
    chunk_heads = heads // CHUNKS
    chunk_spread = chunk_heads * tokens
    channels = heads * head_dim

    def body(slot_ref, len_ref, *refs):
        new_refs = refs[:BATCH]
        (
            win_ref, mat_ref, part_ref, wx_ref, in_ref, last_ref, state_ref, kern_ref, off_ref, skip_ref,
        ) = refs[BATCH : BATCH + 10]
        y_ref, next_ref, tail_ref, y_sc, sems, *exts = refs[BATCH + 10 + len(earlier) :]
        g = pl.program_id(0)
        turn = g % 2

        def copy(i, group, half):
            return pltpu.make_async_copy(
                y_sc.at[half, i], y_ref.at[slot_ref[group * BATCH + i]], sems.at[half, i]
            )

        @pl.when(g >= 2)
        def _():
            for i in range(BATCH):
                copy(i, g - 2, turn).wait()

        owner = lax.broadcasted_iota(jnp.int32, (chunk_spread, width), 0) // tokens
        lane = lax.broadcasted_iota(jnp.int32, (chunk_spread, width), 1) // head_dim
        own = owner == lane
        zero = jnp.zeros((chunk_spread, width), BF16)
        token = lax.broadcasted_iota(jnp.int32, (tokens, width), 0)
        skip_lane = lax.broadcasted_iota(jnp.int32, (1, width), 1) // head_dim
        skip_row = jnp.zeros((1, width), F32)
        for h in range(chunk_heads):
            skip_row = jnp.where(skip_lane == h, skip_ref[k * chunk_heads + h], skip_row)
        for i in range(BATCH):
            c = g * BATCH + i
            ext_sc = exts[i]
            ext_sc[5:8] = win_ref[i].astype(F32)
            ext_sc[8:] = new_refs[i][0].astype(F32)
            tail_ref[i] = jnp.concatenate(
                [ext_sc[pl.ds(len_ref[c] + 5 + n, 1), :] for n in range(3)], axis=0
            ).astype(BF16)
            x = convolve(ext_sc, kern_ref[...], off_ref[...], tokens)
            high, low = halves(x)
            tall_high = jnp.where(own, jnp.concatenate([high] * chunk_heads, axis=0), zero)
            tall_low = jnp.where(own, jnp.concatenate([low] * chunk_heads, axis=0), zero)
            mat = mat_ref[i]
            inside = dot_nn(
                jnp.concatenate([mat, mat[:, :chunk_spread]], axis=1),
                jnp.concatenate([tall_high, tall_high, tall_low], axis=0),
            )
            mixed = inside + part_ref[i] + skip_row * x
            y_sc[turn, i] = jnp.where(token < len_ref[c], mixed, 0.0).astype(BF16)
            copy(i, g, turn).start()
            w_high, w_low = halves(x * wx_ref[i])
            added = dot_tn(jnp.concatenate([w_high, w_high, w_low], axis=0), in_ref[i])
            for h in range(chunk_heads):
                at = k * chunk_heads + h
                next_ref[i, h] = (
                    last_ref[i, at : at + 1, :] * state_ref[i, h].astype(F32)
                    + added[h * head_dim : (h + 1) * head_dim]
                ).astype(BF16)

        @pl.when(g == pl.num_programs(0) - 1)
        def _():
            for i in range(BATCH):
                copy(i, g - 1, 1 - turn).wait()
                copy(i, g, turn).wait()

    def whole(*shape):
        return pl.BlockSpec(shape, lambda g, s, n: (0,) * (len(shape) - 1) + (k,))

    def cut(*shape):
        return pl.BlockSpec((BATCH,) + shape, lambda g, s, n: (g,) + (0,) * (len(shape) - 1) + (k,))

    def at(*shape):
        return pl.BlockSpec((BATCH,) + shape, lambda g, s, n: (g,) + (0,) * len(shape))

    def received(i):
        return pl.BlockSpec((1, tokens, width), lambda g, s, n: (s[g * BATCH + i], 0, 0))

    held = pl.BlockSpec((BATCH, chunk_heads, head_dim, state_dim), lambda g, s, n: (g, k, 0, 0))
    anywhere = pl.BlockSpec(memory_space=pl.ANY)
    operands = [slots, lens, *[fresh] * BATCH, window, mats, parts, loads, in_maps, lasts]
    operands += [state, kernel, offset, skip]
    return pl.pallas_call(
        body,
        out_shape=[
            jax.ShapeDtypeStruct((slot_total, tokens, width), BF16),
            jax.ShapeDtypeStruct(state.shape, BF16),
            jax.ShapeDtypeStruct((sessions, 3, channels), BF16),
        ],
        grid_spec=pltpu.PrefetchScalarGridSpec(
            num_scalar_prefetch=2,
            grid=(sessions // BATCH,),
            in_specs=[received(i) for i in range(BATCH)]
            + [
                cut(3, width),
                cut(tokens, 2 * chunk_spread),
                cut(tokens, width),
                cut(tokens, width),
                at(3 * tokens, state_dim),
                at(heads, 128),
                held,
                whole(4, width),
                whole(1, width),
                pl.BlockSpec(memory_space=pltpu.SMEM),
            ]
            + [anywhere] * len(earlier),
            out_specs=[anywhere, held, cut(3, width)],
            scratch_shapes=[
                pltpu.VMEM((2, BATCH, tokens, width), BF16),
                pltpu.SemaphoreType.DMA((2, BATCH)),
            ]
            + [pltpu.VMEM((tokens + 8, width), F32)] * BATCH,
        ),
        input_output_aliases={len(operands) + i: 1 + i for i in range(len(earlier))},
        compiler_params=params(),
        cost_estimate=cost(sessions * (1 << 24), sessions << 19),
    )(*operands, *earlier)


def block_height(tokens):
    return BLOCK // 2 * tokens + 8


def gate_rows(k, slots, picks, back, gate, adapters, scale, earlier):
    sessions, tokens, _ = gate.shape
    _, _, width = back.shape
    rank = adapters.shape[1] // 2
    height = block_height(tokens)

    def body(slot_ref, pick_ref, *refs):
        backs, downs = refs[:GROUP], refs[GROUP : 2 * GROUP]
        gate_ref, scale_ref = refs[2 * GROUP : 2 * GROUP + 2]
        sum_ref, gated_ref = refs[-2:]
        ones = jnp.ones((8, width), BF16)
        lows, squares = [], []
        for i in range(GROUP):
            gated = backs[i][0].astype(F32) * silu(gate_ref[i].astype(F32))
            gated_ref[i] = gated
            low = dot_nt((gated * scale_ref[...]).astype(BF16), downs[i][0])
            high, rest = halves(gated * gated)
            lows.append(low)
            squares.append(dot_nt(ones, high) + dot_nt(ones, rest))
        for b in range(GROUP // BLOCK):
            rows = [
                jnp.concatenate(lows[i : i + 2], axis=1) for i in range(b * BLOCK, (b + 1) * BLOCK, 2)
            ]
            rows.append(jnp.concatenate(squares[b * BLOCK : (b + 1) * BLOCK], axis=1))
            both = jnp.concatenate(rows, axis=0)
            if earlier:
                both = both + refs[2 * GROUP + 2][b * height : (b + 1) * height]
            sum_ref[b * height : (b + 1) * height] = both

    def returned(i):
        return pl.BlockSpec((1, tokens, width), lambda g, s, a: (s[g * GROUP + i], 0, 0))

    def chosen(i):
        return pl.BlockSpec((1, rank, width), lambda g, s, a: (a[g * GROUP + i], 0, k))

    sums = pl.BlockSpec((GROUP // BLOCK * height, 128), lambda g, s, a: (g, 0))
    return pl.pallas_call(
        body,
        out_shape=[
            jax.ShapeDtypeStruct((sessions // BLOCK * height, 128), F32),
            jax.ShapeDtypeStruct((sessions, tokens, width), F32),
        ],
        grid_spec=pltpu.PrefetchScalarGridSpec(
            num_scalar_prefetch=2,
            grid=(sessions // GROUP,),
            in_specs=[returned(i) for i in range(GROUP)]
            + [chosen(i) for i in range(GROUP)]
            + [
                pl.BlockSpec((GROUP, tokens, width), lambda g, s, a: (g, 0, k)),
                pl.BlockSpec((1, width), lambda g, s, a: (0, k)),
            ]
            + [sums] * len(earlier),
            out_specs=[sums, pl.BlockSpec((GROUP, tokens, width), lambda g, s, a: (g, 0, 0))],
        ),
        compiler_params=params(),
        cost_estimate=cost(sessions * (1 << 22), sessions << 18),
    )(slots, picks, *[back] * GROUP, *[adapters] * GROUP, gate, scale, *earlier)


def finish(picks, gated, totals, adapters, scale, inner):
    sessions, tokens, width = gated[0].shape
    channels = width * CHUNKS
    rank = adapters.shape[1] // 2
    height = block_height(tokens)

    def body(pick_ref, *refs):
        ups, rows = refs[:GROUP], refs[GROUP : GROUP + CHUNKS]
        total_ref, scale_ref, out_ref, delta_ref = refs[GROUP + CHUNKS :]
        spot = lax.broadcasted_iota(jnp.int32, (tokens, tokens), 0) == lax.broadcasted_iota(
            jnp.int32, (tokens, tokens), 1
        )
        for i in range(GROUP):
            start = i // BLOCK * height
            j = i % BLOCK
            line = total_ref[start + height - 8 : start + height - 7, j * tokens : (j + 1) * tokens]
            square = jnp.sum(jnp.where(spot, line, 0.0), axis=1, keepdims=True)
            inverse = lax.rsqrt(square / inner + NORM_EPS)
            first = start + j // 2 * tokens
            low = total_ref[first : first + tokens, j % 2 * rank : (j % 2 + 1) * rank] * inverse
            for k in range(CHUNKS):
                part = slice(k * width, (k + 1) * width)
                out_ref[i, :, part] = (rows[k][i] * inverse * scale_ref[:, part]).astype(BF16)
            delta_ref[i] = dot_nn(low.astype(BF16), ups[i][0]).astype(BF16)

    def chosen(i):
        return pl.BlockSpec((1, rank, channels), lambda g, a: (a[g * GROUP + i], 1, 0))

    out = pl.BlockSpec((GROUP, tokens, channels), lambda g, a: (g, 0, 0))
    return pl.pallas_call(
        body,
        out_shape=[jax.ShapeDtypeStruct((sessions, tokens, channels), BF16)] * 2,
        grid_spec=pltpu.PrefetchScalarGridSpec(
            num_scalar_prefetch=1,
            grid=(sessions // GROUP,),
            in_specs=[chosen(i) for i in range(GROUP)]
            + [pl.BlockSpec((GROUP, tokens, width), lambda g, a: (g, 0, 0))] * CHUNKS
            + [
                pl.BlockSpec((GROUP // BLOCK * height, 128), lambda g, a: (g, 0)),
                pl.BlockSpec((1, channels), lambda g, a: (0, 0)),
            ],
            out_specs=[out, out],
        ),
        compiler_params=params(),
        cost_estimate=cost(sessions * (1 << 22), sessions << 18),
        name="finish",
    )(picks, *[adapters] * GROUP, *gated, totals, scale)


def exchange(value, axis, groups=None):
    return lax.all_to_all(
        value, axis, split_axis=0, concat_axis=0, tiled=True, axis_index_groups=groups
    )


def share_all(value, axis, count, groups=None):
    return exchange(
        jnp.broadcast_to(value[None], (count,) + value.shape).reshape((-1,) + value.shape[1:]), axis, groups
    )


def place(base, length, blocks):
    count = len(blocks)
    shape = blocks[0][0].shape

    def body(base_ref, *refs):
        ins, out_ref = refs[:count], refs[count]
        helds, sems = refs[count + 1 : 2 * count + 1], refs[2 * count + 1]
        loads = [pltpu.make_async_copy(ins[i], helds[i], sems.at[0, i]) for i in range(count)]
        for load in loads:
            load.start()
        stores = []
        for i, (_, behind, part) in enumerate(blocks):
            loads[i].wait()
            target = out_ref.at[(base_ref[0] + (length - behind)) % length]
            if part is not None:
                rest = (slice(None),) * (len(shape) - 2)
                target = target.at[(*rest, slice(part[0], part[1]))]
            stores.append(pltpu.make_async_copy(helds[i], target, sems.at[1, i]))
            stores[i].start()
        for store in stores:
            store.wait()

    return pl.pallas_call(
        body,
        out_shape=jax.ShapeDtypeStruct((length,) + shape, blocks[0][0].dtype),
        in_specs=[pl.BlockSpec(memory_space=pltpu.SMEM)]
        + [pl.BlockSpec(memory_space=pl.ANY)] * count,
        out_specs=pl.BlockSpec(memory_space=pl.ANY),
        scratch_shapes=[pltpu.VMEM(value.shape, value.dtype) for value, _, _ in blocks]
        + [pltpu.SemaphoreType.DMA((2, count))],
        compiler_params=params(),
        cost_estimate=cost(0, 4 * length * blocks[0][0].size),
    )(base.reshape(1), *[value for value, _, _ in blocks])


def shift(value, axis, rings, d):
    pairs = [(ring[i], ring[(i + d) % len(ring)]) for ring in rings for i in range(len(ring))]
    return lax.ppermute(value, axis, pairs)


def everyone(value, axis, rings):
    length = len(rings[0])
    return [(value, 0, None)] + [(shift(value, axis, rings, d), d, None) for d in range(1, length)]


def gather_adapters(block, row, size_z, size_x):
    along_z = [[z * size_x + x for z in range(size_z)] for x in range(size_x)]
    along_x = [[z * size_x + x for x in range(size_x)] for z in range(size_z)]
    size = block.shape[0]
    half = size // 2
    column = place(row // size_x, size_z, everyone(block, "row", along_z))
    parts = [(column, 0, None), (shift(column, "row", along_x, 1), 1, None)]
    if size_x == 4:
        behind = parts[1][0]
        ahead = shift(column, "row", along_x, 3)
        parts.append((ahead, 3, None))
        parts.append((shift(behind[:, :half], "row", along_x, 1), 2, (0, half)))
        parts.append((shift(ahead[:, half:], "row", along_x, 3), 2, (half, size)))
    whole = place(row % size_x, size_x, parts)
    return whole.reshape((size_z * size_x,) + block.shape)


def shards(
    channel_rows_in,
    gate_rows_in,
    map_input_rows,
    step_size_input,
    channel_kernel_weight,
    map_kernel_weight,
    channel_conv_bias,
    map_kernel_bias,
    step_size_bias,
    head_decay_rate,
    head_skip_weight,
    gated_norm_scale,
    scan_state_cache,
    channel_window_cache,
    map_window_cache,
    adapter_down_weight,
    adapter_up_weight,
    session_slot_index,
    lengths,
    session_adapter_index,
):
    sessions, tokens, channels = channel_rows_in.shape
    heads = step_size_input.shape[1]
    rows = lax.axis_size("row")
    sections = lax.axis_size("section")
    row = lax.axis_index("row")
    section = lax.axis_index("section")
    size_x = 4 if rows >= 32 else 2
    size_z = rows // size_x
    side = sections // PAIR
    group_tokens = tokens // side

    local = jnp.arange(sessions, dtype=jnp.int32)
    mine = lax.dynamic_slice_in_dim(session_slot_index, row * sessions, sessions)
    homes = mine // sessions
    sooner = (homes[None, :] == homes[:, None]) & (local[None, :] < local[:, None])
    serve_slots = homes * PAIR + jnp.sum(sooner.astype(jnp.int32), axis=1)
    here = (session_slot_index // sessions == row).astype(jnp.int32).reshape(rows, sessions)
    ahead = jnp.sum(
        jnp.where(local[None, None, :] < local[None, :, None], here[:, None, :], 0), axis=2
    )
    target = (jnp.arange(rows, dtype=jnp.int32)[:, None] * PAIR + ahead).reshape(-1)
    match = session_slot_index[None, :] == (row * sessions + local)[:, None]
    home_slots = jnp.sum(jnp.where(match, target[None, :], 0), axis=1)
    home_lens = jnp.sum(jnp.where(match, lengths[None, :], 0), axis=1)
    adapter = lax.dynamic_slice_in_dim(session_adapter_index, row * sessions, sessions)
    picks = adapter % size_x * size_z + adapter // size_x

    map_slice = lax.dynamic_slice_in_dim(
        map_input_rows, section % side * group_tokens, group_tokens, axis=1
    )
    step_rows = step_size_input.reshape(sessions, heads * tokens).astype(F32)
    sent = pack(
        serve_slots, (section // side).reshape(1), map_slice, step_rows, channel_rows_in, rows * PAIR
    )
    fresh = []
    for k in range(CHUNKS):
        fresh.append(exchange(sent[k], "row"))
    block = jnp.concatenate([adapter_down_weight[0], adapter_up_weight[0]], axis=0)
    block, home_slots, home_lens, picks = lax.optimization_barrier((block, home_slots, home_lens, picks))
    adapters = gather_adapters(block, row, size_z, size_x)
    share = fresh[0].reshape((rows, PAIR) + fresh[0].shape[1:])[:, 0, tokens : tokens + group_tokens]
    maps = place(section, sections, everyone(share, "section", [list(range(sections))]))
    *prepared, map_window_next = prepare(
        home_slots,
        home_lens,
        maps,
        fresh[0],
        map_window_cache,
        scan_state_cache,
        map_kernel_weight,
        map_kernel_bias[None],
        step_size_bias,
        head_decay_rate,
    )
    scale = gated_norm_scale[None]
    back = []
    carried = []
    for k in range(CHUNKS):
        mixed, *carried = mix(
            k,
            home_slots,
            home_lens,
            fresh[k],
            channel_window_cache,
            prepared,
            scan_state_cache,
            channel_kernel_weight,
            channel_conv_bias[None],
            head_skip_weight,
            carried,
        )
        back.append(exchange(mixed, "row"))
    scan_state_next, channel_window_next = carried
    sums = []
    gated = []
    for k in range(CHUNKS):
        total, part = gate_rows(k, serve_slots, picks, back[k], gate_rows_in, adapters, scale, sums)
        sums = [total]
        gated.append(part)
    total = exchange(sums[0], "section")
    total = jnp.sum(total.reshape(sections, -1, 128), axis=0)
    totals = share_all(total, "section", sections)
    mixer_output_rows, adapter_delta = finish(
        picks, gated, totals, adapters, scale, channels * sections
    )
    return (mixer_output_rows, adapter_delta, scan_state_next, channel_window_next, map_window_next)


def solution(mesh):
    split = P("row", None, "section")
    return jax.shard_map(
        shards,
        mesh=mesh,
        in_specs=(
            split,
            split,
            P("row", None, None),
            P("row", "section", None),
            P(None, "section"),
            P(),
            P("section"),
            P(),
            P("section"),
            P("section"),
            P("section"),
            P("section"),
            P("row", "section", None, None),
            split,
            P("row", None, None),
            split,
            split,
            P(),
            P(),
            P(),
        ),
        out_specs=(
            split,
            split,
            P("row", "section", None, None),
            split,
            P("row", None, None),
        ),
        check_vma=False,
    )
```

```python
import jax
import jax.numpy as jnp
from jax import lax
from jax.experimental import pallas as pl
from jax.experimental.pallas import tpu as pltpu
from jax.sharding import PartitionSpec as P


NORM_EPS = 1e-05
PAIR = 2
CHUNKS = 2
GROUP = 16
BATCH = 8

BLOCK = 4

F32 = jnp.float32
BF16 = jnp.bfloat16


def silu(value):
    return value / (1.0 + jnp.exp(-value))


def halves(value):
    high = value.astype(BF16)
    return high, (value - high.astype(F32)).astype(BF16)


def dot_nn(left, right):
    return lax.dot_general(left, right, (((1,), (0,)), ((), ())), preferred_element_type=F32)


def dot_nt(left, right):
    return lax.dot_general(left, right, (((1,), (1,)), ((), ())), preferred_element_type=F32)


def dot_tn(left, right):
    return lax.dot_general(left, right, (((0,), (0,)), ((), ())), preferred_element_type=F32)


def params(megabytes=62):
    return pltpu.CompilerParams(vmem_limit_bytes=megabytes * 1024 * 1024)


def cost(flops, moved, transcendentals=0):
    return pl.CostEstimate(
        flops=int(flops), bytes_accessed=int(moved), transcendentals=int(transcendentals)
    )


def convolve(ext_ref, kernel_rows, offset, tokens):
    summed = offset + kernel_rows[0:1] * ext_ref[5 : 5 + tokens]
    for tap in range(1, 4):
        summed = summed + kernel_rows[tap : tap + 1] * ext_ref[5 + tap : 5 + tap + tokens]
    return silu(summed)


def pack(slots, rank_here, map_slice, steps, rows_in, slot_total):
    sessions, tokens, channels = rows_in.shape
    _, group_tokens, map_width = map_slice.shape
    width = channels // CHUNKS
    extra = max(group_tokens, 8)

    def body(slot_ref, rank_ref, map_ref, step_ref, in_ref, *rest):
        outs = rest[:CHUNKS]
        small_sc, row_sc, step_sc, sems, small_sem = rest[CHUNKS:]

        def copies(q):
            slot = slot_ref[q]
            return [
                pltpu.make_async_copy(
                    in_ref.at[q, :, k * width : (k + 1) * width],
                    outs[k].at[slot, 0:tokens, :],
                    sems.at[k * sessions + q],
                )
                for k in range(CHUNKS)
            ]

        for q in range(sessions):
            for copy in copies(q):
                copy.start()
        heads = step_ref.shape[1]
        raw = step_ref[...].astype(F32)
        row_sc[...] = jnp.concatenate([raw[:, h, :] for h in range(heads)], axis=1)
        for q in range(sessions):
            home = slot_ref[q] // PAIR
            rank = slot_ref[q] % PAIR
            step_sc[home, pl.ds(rank, 1), :] = row_sc[q : q + 1, :]

            @pl.when(rank == rank_ref[0])
            def _():
                small_sc[home, 0, 0:group_tokens] = map_ref[q]

        small_sc[:, 1, 0:8] = step_sc[...].astype(BF16)
        smalls = [
            pltpu.make_async_copy(
                small_sc.at[home], outs[0].at[pl.ds(home * PAIR, PAIR), tokens:, :], small_sem.at[home]
            )
            for home in range(slot_total // PAIR)
        ]
        for copy in smalls:
            copy.start()
        for q in range(sessions):
            for copy in copies(q):
                copy.wait()
        for copy in smalls:
            copy.wait()

    vmem = pl.BlockSpec(memory_space=pltpu.VMEM)
    smem = pl.BlockSpec(memory_space=pltpu.SMEM)
    return pl.pallas_call(
        body,
        out_shape=[
            jax.ShapeDtypeStruct((slot_total, tokens + (extra if k == 0 else 0), width), BF16)
            for k in range(CHUNKS)
        ],
        in_specs=[smem, smem, vmem, vmem, vmem],
        out_specs=[pl.BlockSpec(memory_space=pl.ANY)] * CHUNKS,
        scratch_shapes=[
            pltpu.VMEM((slot_total // PAIR, PAIR, extra, map_width), BF16),
            pltpu.VMEM((sessions, map_width), F32),
            pltpu.VMEM((slot_total // PAIR, 8, map_width), F32),
            pltpu.SemaphoreType.DMA((CHUNKS * sessions,)),
            pltpu.SemaphoreType.DMA((slot_total // PAIR,)),
        ],
        compiler_params=params(),
        cost_estimate=cost(0, 4 << 20),
        name="pack",
    )(slots, rank_here, map_slice, steps, rows_in)


def prepare(slots, lens, maps, fresh, map_window, state, map_kernel, map_bias, bias, decay):
    sessions, heads, head_dim, state_dim = state.shape
    groups, rows, group_tokens, width = maps.shape
    side = groups // PAIR
    tokens = side * group_tokens
    spread = heads * tokens
    channels = heads * head_dim
    chunk_heads = heads // CHUNKS
    chunk_spread = chunk_heads * tokens
    maps = maps.reshape(PAIR, side, rows, group_tokens, width)

    def per_head(values, size):
        lane = lax.broadcasted_iota(jnp.int32, (1, heads * size), 1) // size
        row = jnp.zeros((1, heads * size), F32)
        for h in range(heads):
            row = jnp.where(lane == h, values[h], row)
        return row

    def blocks(columns, size):
        row = lax.broadcasted_iota(jnp.int32, (spread, columns), 0) // tokens
        column = lax.broadcasted_iota(jnp.int32, (spread, columns), 1) // size
        return jnp.where(row == column, 1.0, 0.0).astype(BF16)

    def body(slot_ref, len_ref, *refs):
        map_refs = refs[:BATCH]
        (
            small_ref, win_ref, state_ref, kern_ref, off_ref, bias_ref, rate_ref,
            mat_ref, part_ref, wx_ref, in_ref, last_ref, tail_ref,
            raw_sc, valid_sc, step_sc, log_sc, weight_sc, same_ref, wide_ref,
        ) = refs[BATCH : BATCH + 20]
        exts = refs[BATCH + 20 :]
        lane = lax.broadcasted_iota(jnp.int32, (1, spread), 1) % tokens

        @pl.when(pl.program_id(0) == 0)
        def _():
            same_ref[...] = blocks(spread, tokens)
            wide_ref[...] = blocks(channels, head_dim)
            for s in range(sessions):
                slot = slot_ref[s]
                pair = small_ref[slot // PAIR * PAIR + 1].astype(F32)
                raw_sc[s : s + 1, :] = jnp.where(slot % PAIR == 0, pair[0:1], pair[1:2])
                valid_sc[s : s + 1, :] = jnp.where(lane < len_ref[s], 1.0, 0.0)
            step = jax.nn.softplus(raw_sc[...] + per_head(bias_ref, tokens)) * valid_sc[...]
            fall = -per_head(rate_ref, tokens) * step
            log = fall
            rest = jnp.where(lane < tokens - 1, pltpu.roll(fall, spread - 1, 1), 0.0)
            hop = 1
            while hop < tokens:
                log = log + jnp.where(lane >= hop, pltpu.roll(log, hop, 1), 0.0)
                rest = rest + jnp.where(lane < tokens - hop, pltpu.roll(rest, spread - hop, 1), 0.0)
                hop *= 2
            step_sc[...] = step
            log_sc[...] = log
            weight_sc[...] = jnp.exp(rest) * step

        token = lax.broadcasted_iota(jnp.int32, (tokens, spread), 0)
        within = lax.broadcasted_iota(jnp.int32, (tokens, spread), 1) % tokens
        diagonal = within == token
        causal = within <= token
        final = lax.broadcasted_iota(jnp.int32, (heads, spread), 1) == (
            lax.broadcasted_iota(jnp.int32, (heads, spread), 0) * tokens + tokens - 1
        )
        for i in range(BATCH):
            c = pl.program_id(0) * BATCH + i
            ext_sc = exts[i]
            step = step_sc[pl.ds(c, 1), :]
            log = log_sc[pl.ds(c, 1), :]
            weight = weight_sc[pl.ds(c, 1), :]
            ext_sc[5:8] = win_ref[i].astype(F32)
            ext_sc[8:] = map_refs[i][0, :, 0].astype(F32).reshape(tokens, width)
            tail_ref[i] = jnp.concatenate(
                [ext_sc[pl.ds(len_ref[c] + 5 + n, 1), :] for n in range(3)], axis=0
            ).astype(BF16)
            conv = convolve(ext_sc, kern_ref[...], off_ref[...], tokens)
            in_high, in_low = halves(conv[:, :state_dim])
            out_high, out_low = halves(conv[:, state_dim:])
            in_ref[i] = jnp.concatenate([in_high, in_low, in_high], axis=0)

            log_all = jnp.broadcast_to(log, (tokens, spread))
            spot = jnp.where(diagonal, log_all, 0.0)
            first = spot.astype(BF16)
            second, third = halves(spot - first.astype(F32))
            own = dot_nn(jnp.concatenate([first, second, third], axis=0), same_ref[...])
            own = own[:tokens] + own[tokens : 2 * tokens] + own[2 * tokens :]
            decay = jnp.where(causal, jnp.exp(jnp.where(causal, own - log_all, 0.0)), 0.0)
            keys = jnp.concatenate([jnp.concatenate([in_high, in_low], axis=1)] * heads, axis=0)
            asks = jnp.concatenate(
                [
                    jnp.concatenate([out_high, out_high], axis=1),
                    jnp.concatenate([out_low, jnp.zeros_like(out_low)], axis=1),
                ],
                axis=0,
            )
            scores = dot_nt(asks, keys)
            scores = scores[:tokens] + scores[tokens:]
            high, low = halves(decay * scores * step)
            for k in range(CHUNKS):
                part = slice(k * chunk_spread, (k + 1) * chunk_spread)
                base = 2 * k * chunk_spread
                mat_ref[i, :, base : base + chunk_spread] = high[:, part]
                mat_ref[i, :, base + chunk_spread : base + 2 * chunk_spread] = low[:, part]

            rise = halves(jnp.where(diagonal, jnp.exp(log_all), 0.0))
            load = halves(jnp.where(diagonal, jnp.broadcast_to(weight, (tokens, spread)), 0.0))
            grown = dot_nn(jnp.concatenate([*rise, *load], axis=0), wide_ref[...])
            wx_ref[i] = grown[2 * tokens : 3 * tokens] + grown[3 * tokens :]
            carried = dot_nt(
                jnp.concatenate([out_high, out_low], axis=0), state_ref[i].reshape(channels, state_dim)
            )
            part_ref[i] = (carried[:tokens] + carried[tokens:]) * (
                grown[:tokens] + grown[tokens : 2 * tokens]
            )
            last = jnp.sum(jnp.where(final, jnp.exp(log), 0.0), axis=1, keepdims=True)
            last_ref[i] = jnp.broadcast_to(last, (heads, 128))

    def whole(*shape):
        return pl.BlockSpec(shape, lambda g, s, n: (0,) * len(shape))

    def at(*shape):
        return pl.BlockSpec((BATCH,) + shape, lambda g, s, n: (g,) + (0,) * len(shape))

    def received(i):
        return pl.BlockSpec(
            (1, side, 1, group_tokens, width),
            lambda g, s, n: (s[g * BATCH + i] % PAIR, 0, s[g * BATCH + i] // PAIR, 0, 0),
        )

    return pl.pallas_call(
        body,
        out_shape=[
            jax.ShapeDtypeStruct((sessions, tokens, 2 * spread), BF16),
            jax.ShapeDtypeStruct((sessions, tokens, channels), F32),
            jax.ShapeDtypeStruct((sessions, tokens, channels), F32),
            jax.ShapeDtypeStruct((sessions, 3 * tokens, state_dim), BF16),
            jax.ShapeDtypeStruct((sessions, heads, 128), F32),
            jax.ShapeDtypeStruct((sessions, 3, width), BF16),
        ],
        grid_spec=pltpu.PrefetchScalarGridSpec(
            num_scalar_prefetch=2,
            grid=(sessions // BATCH,),
            in_specs=[received(i) for i in range(BATCH)]
            + [
                pl.BlockSpec((rows * PAIR, 8, width), lambda g, s, n: (0, tokens // 8, 0)),
                at(3, width),
                at(heads, head_dim, state_dim),
                whole(4, width),
                whole(1, width),
                pl.BlockSpec(memory_space=pltpu.SMEM),
                pl.BlockSpec(memory_space=pltpu.SMEM),
            ],
            out_specs=[
                at(tokens, 2 * spread),
                at(tokens, channels),
                at(tokens, channels),
                at(3 * tokens, state_dim),
                at(heads, 128),
                at(3, width),
            ],
            scratch_shapes=[pltpu.VMEM((sessions, spread), F32)] * 5
            + [pltpu.VMEM((spread, spread), BF16), pltpu.VMEM((spread, channels), BF16)]
            + [pltpu.VMEM((tokens + 8, width), F32)] * BATCH,
        ),
        compiler_params=params(),
        cost_estimate=cost(sessions * (1 << 25), sessions << 19),
        name="prepare",
    )(
        slots, lens, *[maps] * BATCH, fresh, map_window, state, map_kernel, map_bias, bias, decay
    )


def mix(k, slots, lens, fresh, window, prepared, state, kernel, offset, skip, earlier):
    mats, parts, loads, in_maps, lasts = prepared
    slot_total, _, width = fresh.shape
    tokens = mats.shape[1]
    sessions, heads, head_dim, state_dim = state.shape
    chunk_heads = heads // CHUNKS
    chunk_spread = chunk_heads * tokens
    channels = heads * head_dim

    def body(slot_ref, len_ref, *refs):
        new_refs = refs[:BATCH]
        (
            win_ref, mat_ref, part_ref, wx_ref, in_ref, last_ref, state_ref, kern_ref, off_ref, skip_ref,
        ) = refs[BATCH : BATCH + 10]
        y_ref, next_ref, tail_ref, y_sc, sems, *exts = refs[BATCH + 10 + len(earlier) :]
        g = pl.program_id(0)
        turn = g % 2

        def copy(i, group, half):
            return pltpu.make_async_copy(
                y_sc.at[half, i], y_ref.at[slot_ref[group * BATCH + i]], sems.at[half, i]
            )

        @pl.when(g >= 2)
        def _():
            for i in range(BATCH):
                copy(i, g - 2, turn).wait()

        owner = lax.broadcasted_iota(jnp.int32, (chunk_spread, width), 0) // tokens
        lane = lax.broadcasted_iota(jnp.int32, (chunk_spread, width), 1) // head_dim
        own = owner == lane
        zero = jnp.zeros((chunk_spread, width), BF16)
        token = lax.broadcasted_iota(jnp.int32, (tokens, width), 0)
        skip_lane = lax.broadcasted_iota(jnp.int32, (1, width), 1) // head_dim
        skip_row = jnp.zeros((1, width), F32)
        for h in range(chunk_heads):
            skip_row = jnp.where(skip_lane == h, skip_ref[k * chunk_heads + h], skip_row)
        for i in range(BATCH):
            c = g * BATCH + i
            ext_sc = exts[i]
            ext_sc[5:8] = win_ref[i].astype(F32)
            ext_sc[8:] = new_refs[i][0].astype(F32)
            tail_ref[i] = jnp.concatenate(
                [ext_sc[pl.ds(len_ref[c] + 5 + n, 1), :] for n in range(3)], axis=0
            ).astype(BF16)
            x = convolve(ext_sc, kern_ref[...], off_ref[...], tokens)
            high, low = halves(x)
            tall_high = jnp.where(own, jnp.concatenate([high] * chunk_heads, axis=0), zero)
            tall_low = jnp.where(own, jnp.concatenate([low] * chunk_heads, axis=0), zero)
            mat = mat_ref[i]
            inside = dot_nn(
                jnp.concatenate([mat, mat[:, :chunk_spread]], axis=1),
                jnp.concatenate([tall_high, tall_high, tall_low], axis=0),
            )
            mixed = inside + part_ref[i] + skip_row * x
            y_sc[turn, i] = jnp.where(token < len_ref[c], mixed, 0.0).astype(BF16)
            copy(i, g, turn).start()
            w_high, w_low = halves(x * wx_ref[i])
            added = dot_tn(jnp.concatenate([w_high, w_high, w_low], axis=0), in_ref[i])
            for h in range(chunk_heads):
                at = k * chunk_heads + h
                next_ref[i, h] = (
                    last_ref[i, at : at + 1, :] * state_ref[i, h].astype(F32)
                    + added[h * head_dim : (h + 1) * head_dim]
                ).astype(BF16)

        @pl.when(g == pl.num_programs(0) - 1)
        def _():
            for i in range(BATCH):
                copy(i, g - 1, 1 - turn).wait()
                copy(i, g, turn).wait()

    def whole(*shape):
        return pl.BlockSpec(shape, lambda g, s, n: (0,) * (len(shape) - 1) + (k,))

    def cut(*shape):
        return pl.BlockSpec((BATCH,) + shape, lambda g, s, n: (g,) + (0,) * (len(shape) - 1) + (k,))

    def at(*shape):
        return pl.BlockSpec((BATCH,) + shape, lambda g, s, n: (g,) + (0,) * len(shape))

    def received(i):
        return pl.BlockSpec((1, tokens, width), lambda g, s, n: (s[g * BATCH + i], 0, 0))

    held = pl.BlockSpec((BATCH, chunk_heads, head_dim, state_dim), lambda g, s, n: (g, k, 0, 0))
    anywhere = pl.BlockSpec(memory_space=pl.ANY)
    operands = [slots, lens, *[fresh] * BATCH, window, mats, parts, loads, in_maps, lasts]
    operands += [state, kernel, offset, skip]
    return pl.pallas_call(
        body,
        out_shape=[
            jax.ShapeDtypeStruct((slot_total, tokens, width), BF16),
            jax.ShapeDtypeStruct(state.shape, BF16),
            jax.ShapeDtypeStruct((sessions, 3, channels), BF16),
        ],
        grid_spec=pltpu.PrefetchScalarGridSpec(
            num_scalar_prefetch=2,
            grid=(sessions // BATCH,),
            in_specs=[received(i) for i in range(BATCH)]
            + [
                cut(3, width),
                cut(tokens, 2 * chunk_spread),
                cut(tokens, width),
                cut(tokens, width),
                at(3 * tokens, state_dim),
                at(heads, 128),
                held,
                whole(4, width),
                whole(1, width),
                pl.BlockSpec(memory_space=pltpu.SMEM),
            ]
            + [anywhere] * len(earlier),
            out_specs=[anywhere, held, cut(3, width)],
            scratch_shapes=[
                pltpu.VMEM((2, BATCH, tokens, width), BF16),
                pltpu.SemaphoreType.DMA((2, BATCH)),
            ]
            + [pltpu.VMEM((tokens + 8, width), F32)] * BATCH,
        ),
        input_output_aliases={len(operands) + i: 1 + i for i in range(len(earlier))},
        compiler_params=params(),
        cost_estimate=cost(sessions * (1 << 24), sessions << 19),
    )(*operands, *earlier)


def block_height(tokens):
    return BLOCK // 2 * tokens + 8


def gate_rows(k, slots, picks, back, gate, adapters, scale, earlier):
    sessions, tokens, _ = gate.shape
    _, _, width = back.shape
    rank = adapters.shape[1] // 2
    height = block_height(tokens)

    def body(slot_ref, pick_ref, *refs):
        backs, downs = refs[:GROUP], refs[GROUP : 2 * GROUP]
        gate_ref, scale_ref = refs[2 * GROUP : 2 * GROUP + 2]
        sum_ref, gated_ref = refs[-2:]
        ones = jnp.ones((8, width), BF16)
        lows, squares = [], []
        for i in range(GROUP):
            gated = backs[i][0].astype(F32) * silu(gate_ref[i].astype(F32))
            gated_ref[i] = gated
            low = dot_nt((gated * scale_ref[...]).astype(BF16), downs[i][0])
            high, rest = halves(gated * gated)
            lows.append(low)
            squares.append(dot_nt(ones, high) + dot_nt(ones, rest))
        for b in range(GROUP // BLOCK):
            rows = [
                jnp.concatenate(lows[i : i + 2], axis=1) for i in range(b * BLOCK, (b + 1) * BLOCK, 2)
            ]
            rows.append(jnp.concatenate(squares[b * BLOCK : (b + 1) * BLOCK], axis=1))
            both = jnp.concatenate(rows, axis=0)
            if earlier:
                both = both + refs[2 * GROUP + 2][b * height : (b + 1) * height]
            sum_ref[b * height : (b + 1) * height] = both

    def returned(i):
        return pl.BlockSpec((1, tokens, width), lambda g, s, a: (s[g * GROUP + i], 0, 0))

    def chosen(i):
        return pl.BlockSpec((1, rank, width), lambda g, s, a: (a[g * GROUP + i], 0, k))

    sums = pl.BlockSpec((GROUP // BLOCK * height, 128), lambda g, s, a: (g, 0))
    return pl.pallas_call(
        body,
        out_shape=[
            jax.ShapeDtypeStruct((sessions // BLOCK * height, 128), F32),
            jax.ShapeDtypeStruct((sessions, tokens, width), F32),
        ],
        grid_spec=pltpu.PrefetchScalarGridSpec(
            num_scalar_prefetch=2,
            grid=(sessions // GROUP,),
            in_specs=[returned(i) for i in range(GROUP)]
            + [chosen(i) for i in range(GROUP)]
            + [
                pl.BlockSpec((GROUP, tokens, width), lambda g, s, a: (g, 0, k)),
                pl.BlockSpec((1, width), lambda g, s, a: (0, k)),
            ]
            + [sums] * len(earlier),
            out_specs=[sums, pl.BlockSpec((GROUP, tokens, width), lambda g, s, a: (g, 0, 0))],
        ),
        compiler_params=params(),
        cost_estimate=cost(sessions * (1 << 22), sessions << 18),
    )(slots, picks, *[back] * GROUP, *[adapters] * GROUP, gate, scale, *earlier)


def finish(picks, gated, totals, adapters, scale, inner):
    sessions, tokens, width = gated[0].shape
    channels = width * CHUNKS
    rank = adapters.shape[1] // 2
    height = block_height(tokens)

    def body(pick_ref, *refs):
        ups, rows = refs[:GROUP], refs[GROUP : GROUP + CHUNKS]
        total_ref, scale_ref, out_ref, delta_ref = refs[GROUP + CHUNKS :]
        spot = lax.broadcasted_iota(jnp.int32, (tokens, tokens), 0) == lax.broadcasted_iota(
            jnp.int32, (tokens, tokens), 1
        )
        for i in range(GROUP):
            start = i // BLOCK * height
            j = i % BLOCK
            line = total_ref[start + height - 8 : start + height - 7, j * tokens : (j + 1) * tokens]
            square = jnp.sum(jnp.where(spot, line, 0.0), axis=1, keepdims=True)
            inverse = lax.rsqrt(square / inner + NORM_EPS)
            first = start + j // 2 * tokens
            low = total_ref[first : first + tokens, j % 2 * rank : (j % 2 + 1) * rank] * inverse
            for k in range(CHUNKS):
                part = slice(k * width, (k + 1) * width)
                out_ref[i, :, part] = (rows[k][i] * inverse * scale_ref[:, part]).astype(BF16)
            delta_ref[i] = dot_nn(low.astype(BF16), ups[i][0]).astype(BF16)

    def chosen(i):
        return pl.BlockSpec((1, rank, channels), lambda g, a: (a[g * GROUP + i], 1, 0))

    out = pl.BlockSpec((GROUP, tokens, channels), lambda g, a: (g, 0, 0))
    return pl.pallas_call(
        body,
        out_shape=[jax.ShapeDtypeStruct((sessions, tokens, channels), BF16)] * 2,
        grid_spec=pltpu.PrefetchScalarGridSpec(
            num_scalar_prefetch=1,
            grid=(sessions // GROUP,),
            in_specs=[chosen(i) for i in range(GROUP)]
            + [pl.BlockSpec((GROUP, tokens, width), lambda g, a: (g, 0, 0))] * CHUNKS
            + [
                pl.BlockSpec((GROUP // BLOCK * height, 128), lambda g, a: (g, 0)),
                pl.BlockSpec((1, channels), lambda g, a: (0, 0)),
            ],
            out_specs=[out, out],
        ),
        compiler_params=params(),
        cost_estimate=cost(sessions * (1 << 22), sessions << 18),
        name="finish",
    )(picks, *[adapters] * GROUP, *gated, totals, scale)


def exchange(value, axis, groups=None):
    return lax.all_to_all(
        value, axis, split_axis=0, concat_axis=0, tiled=True, axis_index_groups=groups
    )


def share_all(value, axis, count, groups=None):
    return exchange(
        jnp.broadcast_to(value[None], (count,) + value.shape).reshape((-1,) + value.shape[1:]), axis, groups
    )


def place(base, length, blocks):
    count = len(blocks)
    shape = blocks[0][0].shape

    def body(base_ref, *refs):
        ins, out_ref = refs[:count], refs[count]
        helds, sems = refs[count + 1 : 2 * count + 1], refs[2 * count + 1]
        loads = [pltpu.make_async_copy(ins[i], helds[i], sems.at[0, i]) for i in range(count)]
        for load in loads:
            load.start()
        stores = []
        for i, (_, behind, part) in enumerate(blocks):
            loads[i].wait()
            target = out_ref.at[(base_ref[0] + (length - behind)) % length]
            if part is not None:
                rest = (slice(None),) * (len(shape) - 2)
                target = target.at[(*rest, slice(part[0], part[1]))]
            stores.append(pltpu.make_async_copy(helds[i], target, sems.at[1, i]))
            stores[i].start()
        for store in stores:
            store.wait()

    return pl.pallas_call(
        body,
        out_shape=jax.ShapeDtypeStruct((length,) + shape, blocks[0][0].dtype),
        in_specs=[pl.BlockSpec(memory_space=pltpu.SMEM)]
        + [pl.BlockSpec(memory_space=pl.ANY)] * count,
        out_specs=pl.BlockSpec(memory_space=pl.ANY),
        scratch_shapes=[pltpu.VMEM(value.shape, value.dtype) for value, _, _ in blocks]
        + [pltpu.SemaphoreType.DMA((2, count))],
        compiler_params=params(),
        cost_estimate=cost(0, 4 * length * blocks[0][0].size),
    )(base.reshape(1), *[value for value, _, _ in blocks])


def shift(value, axis, rings, d):
    pairs = [(ring[i], ring[(i + d) % len(ring)]) for ring in rings for i in range(len(ring))]
    return lax.ppermute(value, axis, pairs)


def everyone(value, axis, rings):
    length = len(rings[0])
    return [(value, 0, None)] + [(shift(value, axis, rings, d), d, None) for d in range(1, length)]


def gather_adapters(block, row, size_z, size_x):
    along_z = [[z * size_x + x for z in range(size_z)] for x in range(size_x)]
    along_x = [[z * size_x + x for x in range(size_x)] for z in range(size_z)]
    size = block.shape[0]
    half = size // 2
    column = place(row // size_x, size_z, everyone(block, "row", along_z))
    parts = [(column, 0, None), (shift(column, "row", along_x, 1), 1, None)]
    if size_x == 4:
        behind = parts[1][0]
        ahead = shift(column, "row", along_x, 3)
        parts.append((ahead, 3, None))
        parts.append((shift(behind[:, :half], "row", along_x, 1), 2, (0, half)))
        parts.append((shift(ahead[:, half:], "row", along_x, 3), 2, (half, size)))
    whole = place(row % size_x, size_x, parts)
    return whole.reshape((size_z * size_x,) + block.shape)


def shards(
    channel_rows_in,
    gate_rows_in,
    map_input_rows,
    step_size_input,
    channel_kernel_weight,
    map_kernel_weight,
    channel_conv_bias,
    map_kernel_bias,
    step_size_bias,
    head_decay_rate,
    head_skip_weight,
    gated_norm_scale,
    scan_state_cache,
    channel_window_cache,
    map_window_cache,
    adapter_down_weight,
    adapter_up_weight,
    session_slot_index,
    lengths,
    session_adapter_index,
):
    sessions, tokens, channels = channel_rows_in.shape
    rows = lax.axis_size("row")
    sections = lax.axis_size("section")
    row = lax.axis_index("row")
    section = lax.axis_index("section")
    size_x = 4 if rows >= 32 else 2
    size_z = rows // size_x
    side = sections // PAIR
    group_tokens = tokens // side

    local = jnp.arange(sessions, dtype=jnp.int32)
    mine = lax.dynamic_slice_in_dim(session_slot_index, row * sessions, sessions)
    homes = mine // sessions
    sooner = (homes[None, :] == homes[:, None]) & (local[None, :] < local[:, None])
    serve_slots = homes * PAIR + jnp.sum(sooner.astype(jnp.int32), axis=1)
    here = (session_slot_index // sessions == row).astype(jnp.int32).reshape(rows, sessions)
    ahead = jnp.sum(
        jnp.where(local[None, None, :] < local[None, :, None], here[:, None, :], 0), axis=2
    )
    target = (jnp.arange(rows, dtype=jnp.int32)[:, None] * PAIR + ahead).reshape(-1)
    match = session_slot_index[None, :] == (row * sessions + local)[:, None]
    home_slots = jnp.sum(jnp.where(match, target[None, :], 0), axis=1)
    home_lens = jnp.sum(jnp.where(match, lengths[None, :], 0), axis=1)
    adapter = lax.dynamic_slice_in_dim(session_adapter_index, row * sessions, sessions)
    picks = adapter % size_x * size_z + adapter // size_x

    map_slice = lax.dynamic_slice_in_dim(
        map_input_rows, section % side * group_tokens, group_tokens, axis=1
    )
    sent = pack(
        serve_slots, (section // side).reshape(1), map_slice, step_size_input, channel_rows_in, rows * PAIR
    )
    fresh = []
    for k in range(CHUNKS):
        fresh.append(exchange(sent[k], "row"))
    block = jnp.concatenate([adapter_down_weight[0], adapter_up_weight[0]], axis=0)
    block, home_slots, home_lens, picks = lax.optimization_barrier((block, home_slots, home_lens, picks))
    adapters = gather_adapters(block, row, size_z, size_x)
    share = fresh[0].reshape((rows, PAIR) + fresh[0].shape[1:])[:, 0, tokens : tokens + group_tokens]
    maps = place(section, sections, everyone(share, "section", [list(range(sections))]))
    *prepared, map_window_next = prepare(
        home_slots,
        home_lens,
        maps,
        fresh[0],
        map_window_cache,
        scan_state_cache,
        map_kernel_weight,
        map_kernel_bias[None],
        step_size_bias,
        head_decay_rate,
    )
    scale = gated_norm_scale[None]
    back = []
    carried = []
    for k in range(CHUNKS):
        mixed, *carried = mix(
            k,
            home_slots,
            home_lens,
            fresh[k],
            channel_window_cache,
            prepared,
            scan_state_cache,
            channel_kernel_weight,
            channel_conv_bias[None],
            head_skip_weight,
            carried,
        )
        back.append(exchange(mixed, "row"))
    scan_state_next, channel_window_next = carried
    sums = []
    gated = []
    for k in range(CHUNKS):
        total, part = gate_rows(k, serve_slots, picks, back[k], gate_rows_in, adapters, scale, sums)
        sums = [total]
        gated.append(part)
    total = exchange(sums[0], "section")
    total = jnp.sum(total.reshape(sections, -1, 128), axis=0)
    totals = share_all(total, "section", sections)
    mixer_output_rows, adapter_delta = finish(
        picks, gated, totals, adapters, scale, channels * sections
    )
    return (mixer_output_rows, adapter_delta, scan_state_next, channel_window_next, map_window_next)


def solution(mesh):
    split = P("row", None, "section")
    return jax.shard_map(
        shards,
        mesh=mesh,
        in_specs=(
            split,
            split,
            P("row", None, None),
            P("row", "section", None),
            P(None, "section"),
            P(),
            P("section"),
            P(),
            P("section"),
            P("section"),
            P("section"),
            P("section"),
            P("row", "section", None, None),
            split,
            P("row", None, None),
            split,
            split,
            P(),
            P(),
            P(),
        ),
        out_specs=(
            split,
            split,
            P("row", "section", None, None),
            split,
            P("row", None, None),
        ),
        check_vma=False,
    )
```
